256 devices in a mesh: seq: 32 (over z, y), mp: 4 (over x), req: 2 (over core).
Axes of the slice: x: 4, y: 4, z: 8, core: 2. Of those that a mesh axis runs over, the one named last changes fastest.
Arguments:
- hidden: bfloat16 [2, 8192, 3072], P('req', 'seq', 'mp'), may hold values from -6 to 6
- norm_gain: bfloat16 [3072], replicated, may hold values from 0.5 to 1.5
- w_query: bfloat16 [3072, 1024], P(None, 'mp'), may hold values from -0.109375 to 0.109375
- w_keyval: bfloat16 [3072, 512], P(None, 'mp'), may hold values from -0.109375 to 0.109375
- w_attn_out: bfloat16 [1024, 3072], P('mp'), may hold values from -1.5 to 1.5
- w_inner: bfloat16 [3072, 2, 1536], P(None, None, 'mp'), may hold values from -0.109375 to 0.109375
- w_bc: bfloat16 [3072, 512], P(None, 'mp'), may hold values from -0.109375 to 0.109375
- w_dt: bfloat16 [3072, 12], P(None, 'mp'), may hold values from -0.109375 to 0.109375
- dt_bias: float32 [12], P('mp'), may hold values from -4 to 0
- a_log: float32 [12], P('mp'), may hold values from -12 to 0
- d_skip: float32 [12], P('mp'), may hold values from 0.1 to 10
- conv_x: bfloat16 [4, 1536], P(None, 'mp'), may hold values from -3 to 3
- conv_bc: bfloat16 [4, 512], replicated, may hold values from -3 to 3
- mamba_gain: bfloat16 [1536], P('mp'), may hold values from 0.5 to 1.5
- w_mamba_out: bfloat16 [1536, 3072], P('mp'), may hold values from -0.15625 to 0.15625
- cache: bfloat16 [2, 8192, 512], P('req', 'seq', 'mp'), may hold values from -70 to 70, as said below
- cache_len: int32 [2], P('req'), may hold values from 256 to 8192
- tail_x: bfloat16 [2, 3, 1536], P('req', None, 'mp'), may hold values from -6 to 6
- tail_bc: bfloat16 [2, 3, 512], P('req'), may hold values from -6 to 6
- ssm_init: float32 [2, 12, 128, 256], P('req', 'mp'), may hold values from -6 to 6
Outputs:
- layer_out: bfloat16 [2, 8192, 3072], P('req', 'seq', 'mp')
- new_keyval: bfloat16 [2, 8192, 512], P('req', 'seq', 'mp')
- block_states: float32 [2, 32, 12, 128, 256], P('req', 'seq', 'mp')
The draws below stay inside these ranges and needn't reach their ends.
Inputs may be any that keep to these rules, and one draw needn't show every extreme that they name: Rows of the cache at or past cache_len are unused.
All inputs are finite; a program needn't handle non-finite values.
Results may differ from the reference program's by a relative error of at most 0.0097.
Values may be sent and summed in bfloat16 or wider, within the bound.
A program may use at most 192 MiB of HBM per device.

```python
import math
import jax
import jax.numpy as jnp
import numpy as np
from jax import lax

D = 3072
HD = 128
QH = 8
KVH = 2
MH = 12
NS = 256
CONV = 4
NEW_DEV = 256
CACHE_DEV = 256
REQS = 2
SEQ_BLOCKS = 32
NEW = 8192
CACHE = 8192


def draw_cache(key, part):
    first_key = jax.random.fold_in(key, 0)
    shape = (REQS, CACHE, 2 * KVH * HD)
    column = jnp.arange(2 * KVH * HD)
    is_key = (column // HD % 2 == 0)[None, None, :]
    scales = jnp.where(is_key, 2.0, 1.0)
    base = jnp.clip(jax.random.normal(first_key, shape, jnp.float32), -4.0, 4.0) * scales
    return base.astype(jnp.bfloat16)


def block_levels(rng, dims, cuts, least, top_value):
    factor_of, own = 1.0, jax.random.fold_in(rng, 6)
    for axis_at, shards_of in cuts:
        steps = jnp.exp(jax.random.uniform(jax.random.fold_in(own, axis_at), (shards_of,), jnp.float32, least / len(cuts), top_value / len(cuts)))
        factor_of = factor_of * jnp.repeat(steps, dims[axis_at] // shards_of).reshape([-1 if axis == axis_at else 1 for axis in range(len(dims))])
    return factor_of


def gaussian(rng, extent, width, limit, cuts=(), held_as=jnp.bfloat16):
    loudness = block_levels(rng, extent, cuts, -0.22, 0.18) if cuts else 1.0
    entries = jax.random.normal(rng, extent, jnp.float32) * width * loudness
    return jnp.minimum(jnp.maximum(entries, -limit), limit).astype(held_as)


def setup_inputs(seed: int = 0) -> dict:
    splits = jax.random.split(jax.random.key(seed), 21)
    hidden = gaussian(splits[0], (REQS, NEW, D), 1.0, 6.0, ((0, 2), (1, 32), (2, 4)))
    norm_gain = jnp.clip(1.0 + 0.1 * jax.random.normal(splits[1], (D,), jnp.float32), 0.5, 1.5).astype(jnp.bfloat16)
    w_query = gaussian(splits[2], (D, QH * HD), D ** -0.5, 0.109375, ((1, 4),))
    w_keyval = gaussian(splits[3], (D, 2 * KVH * HD), D ** -0.5, 0.109375, ((1, 4),))
    w_attn_out = gaussian(splits[4], (QH * HD, D), (HD // 8) ** -0.5, 1.5, ((0, 4),))
    w_inner = gaussian(splits[5], (D, 2, MH * HD), D ** -0.5, 0.109375, ((2, 4),))
    w_bc = gaussian(splits[6], (D, 2 * NS), D ** -0.5, 0.109375, ((1, 4),))
    w_dt = gaussian(splits[7], (D, MH), D ** -0.5, 0.109375, ((1, 4),))
    dt_bias = jnp.clip(-4.0 + 4.0 * jax.random.uniform(splits[8], (MH,), jnp.float32) ** block_levels(splits[8], (MH,), ((0, 4),), -0.2, 0.2), -4.0, 0.0)
    a_log = jnp.clip(-12.0 + 12.0 * jax.random.uniform(splits[9], (MH,), jnp.float32) ** block_levels(splits[9], (MH,), ((0, 4),), -0.2, 0.2), -12.0, 0.0)
    d_skip = jnp.clip(jnp.exp(math.log(10.0) - 4.6051702 * jax.random.uniform(splits[10], (MH,), jnp.float32) ** block_levels(splits[10], (MH,), ((0, 4),), -0.2, 0.2)), 0.1, 10.0)
    conv_x = gaussian(splits[11], (CONV, MH * HD), CONV ** -0.5, 3.0, ((1, 4),))
    conv_bc = gaussian(splits[12], (CONV, 2 * NS), CONV ** -0.5, 3.0)
    mamba_gain = jnp.clip(1.0 + 0.1 * jax.random.normal(splits[13], (MH * HD,), jnp.float32), 0.5, 1.5).astype(jnp.bfloat16)
    w_mamba_out = gaussian(splits[14], (MH * HD, D), (MH * HD) ** -0.5, 0.15625, ((0, 4),))
    cache = draw_cache(jax.random.fold_in(splits[20], 71), 0)
    cache_len = jax.random.randint(splits[16], (REQS,), CACHE_DEV, CACHE + 1).astype(jnp.int32)
    tail_x = gaussian(splits[17], (REQS, CONV - 1, MH * HD), 1.0, 6.0, ((0, 2), (2, 4)))
    tail_bc = gaussian(splits[18], (REQS, CONV - 1, 2 * NS), 1.0, 6.0, ((0, 2),))
    ssm_init = gaussian(splits[19], (REQS, MH, HD, NS), 1.0, 6.0, ((0, 2), (1, 4)), jnp.float32)
    return {"hidden": hidden, "norm_gain": norm_gain, "w_query": w_query, "w_keyval": w_keyval, "w_attn_out": w_attn_out, "w_inner": w_inner, "w_bc": w_bc, "w_dt": w_dt, "dt_bias": dt_bias, "a_log": a_log, "d_skip": d_skip, "conv_x": conv_x, "conv_bc": conv_bc, "mamba_gain": mamba_gain, "w_mamba_out": w_mamba_out, "cache": cache, "cache_len": cache_len, "tail_x": tail_x, "tail_bc": tail_bc, "ssm_init": ssm_init}


epsilon = 1e-05
rope_base = 100000000000.0
negative = -1e+30

def rotate(values, positions):
    half = HD // 2
    freqs = rope_base ** (-jnp.arange(half, dtype=jnp.float32) * 2.0 / HD)
    angles = positions.astype(jnp.float32)[:, None] * freqs[None, :]
    cosine = jnp.cos(angles)[:, None, :]
    sine = jnp.sin(angles)[:, None, :]
    first = values[..., :half]
    second = values[..., half:]
    return jnp.concatenate([first * cosine - second * sine, second * cosine + first * sine], axis=-1)

def rms_scale(values):
    mean_sq = lax.optimization_barrier(jnp.mean(values * values, axis=-1, keepdims=True))
    return values * lax.rsqrt(mean_sq + epsilon)

def causal_conv(tail, inputs, taps):
    padded = jnp.concatenate([tail, inputs], axis=0).astype(jnp.float32)
    count = inputs.shape[0]
    total = jnp.zeros(inputs.shape, jnp.float32)
    for offset in range(CONV):
        total = total + taps[offset].astype(jnp.float32)[None, :] * padded[offset:offset + count]
    return jax.nn.silu(total)

def one_request(hidden_r, norm_gain, w_query, w_keyval, w_attn_out, w_inner, w_bc, w_dt, dt_bias, a_log, d_skip, conv_x, conv_bc, mamba_gain, w_mamba_out, cache_r, length, tail_xr, tail_bcr, init_r):
    high = lax.Precision.HIGHEST
    normed = (rms_scale(hidden_r.astype(jnp.float32)) * norm_gain.astype(jnp.float32)).astype(jnp.bfloat16)
    positions = length + jnp.arange(NEW, dtype=jnp.int32)
    query = rotate(jnp.dot(normed, w_query, preferred_element_type=jnp.float32).reshape(NEW, QH, HD), positions)
    query = query.astype(jnp.bfloat16)
    projected = jnp.dot(normed, w_keyval, preferred_element_type=jnp.float32).reshape(NEW, 2 * KVH, HD)
    is_key = (jnp.arange(2 * KVH) % 2 == 0)[None, :, None]
    new_kv = jnp.where(is_key, rotate(projected, positions), projected).astype(jnp.bfloat16)
    new_flat = new_kv.reshape(NEW, 2 * KVH * HD)
    bc_proj = jnp.dot(normed, w_bc, preferred_element_type=jnp.float32).astype(jnp.bfloat16)
    inner = jnp.einsum('td,dkc->tkc', normed.astype(jnp.float32), w_inner.astype(jnp.float32)).astype(jnp.bfloat16)
    gate_z = inner[:, 0]
    x_in = inner[:, 1]
    x_conv = causal_conv(tail_xr, x_in, conv_x).reshape(NEW, MH, HD)
    bc_conv = causal_conv(tail_bcr, bc_proj, conv_bc)
    b_mat = bc_conv[:, :NS]
    c_mat = bc_conv[:, NS:]
    step_size = jax.nn.softplus(jnp.dot(normed, w_dt, preferred_element_type=jnp.float32) + dt_bias.astype(jnp.float32))
    log_decay = -step_size * jnp.exp(a_log.astype(jnp.float32))[None, :]

    def token(state, inputs):
        decay_t, step_t, x_t, b_t, c_t = inputs
        state = jnp.exp(decay_t)[:, None, None] * state + (step_t[:, None] * x_t)[:, :, None] * b_t[None, None, :]
        return (state, jnp.einsum('hpn,n->hp', state, c_t, precision=high))

    def block(state, inputs):
        state, outputs = lax.scan(token, state, inputs)
        return (state, (outputs, state))
    blocked = (log_decay.reshape(SEQ_BLOCKS, NEW_DEV, MH), step_size.reshape(SEQ_BLOCKS, NEW_DEV, MH), x_conv.reshape(SEQ_BLOCKS, NEW_DEV, MH, HD), b_mat.reshape(SEQ_BLOCKS, NEW_DEV, NS), c_mat.reshape(SEQ_BLOCKS, NEW_DEV, NS))
    final_state, (outputs, states) = lax.scan(block, init_r.astype(jnp.float32), blocked)
    mamba_y = outputs.reshape(NEW, MH, HD) + d_skip.astype(jnp.float32)[None, :, None] * x_conv
    gated = mamba_y * jax.nn.silu(gate_z.astype(jnp.float32).reshape(NEW, MH, HD))
    mixed = (rms_scale(gated).reshape(NEW, MH * HD) * mamba_gain.astype(jnp.float32)).astype(jnp.bfloat16)
    cache_heads = cache_r.reshape(CACHE, 2 * KVH, HD)
    keys = jnp.concatenate([cache_heads[:, 0::2], new_kv[:, 0::2]], axis=0).astype(jnp.float32)
    values = jnp.concatenate([cache_heads[:, 1::2], new_kv[:, 1::2]], axis=0).astype(jnp.float32)
    group_of = np.arange(QH) // (QH // KVH)
    keys_head = jnp.transpose(keys, (1, 0, 2))[group_of]
    values_head = jnp.transpose(values, (1, 0, 2))[group_of]
    cache_ok = jnp.arange(CACHE, dtype=jnp.int32) < length
    scale = 1.0 / math_sqrt(HD)

    def attend(index):
        start = index * NEW_DEV
        query_block = lax.dynamic_slice_in_dim(query, start, NEW_DEV, 0).astype(jnp.float32)
        query_index = start + jnp.arange(NEW_DEV, dtype=jnp.int32)
        new_ok = jnp.arange(NEW, dtype=jnp.int32)[None, :] <= query_index[:, None]
        valid = jnp.concatenate([jnp.broadcast_to(cache_ok[None, :], (NEW_DEV, CACHE)), new_ok], axis=1)
        scores = jnp.einsum('qhd,hkd->hqk', query_block, keys_head) * scale
        masked = jnp.where(valid[None], scores, negative)
        top = lax.optimization_barrier(jnp.max(masked, axis=-1, keepdims=True))
        weights = jnp.where(valid[None], jnp.exp(masked - top), 0.0)
        rounded = lax.optimization_barrier(weights.astype(jnp.bfloat16)).astype(jnp.float32)
        summed = jnp.einsum('hqk,hkd->qhd', rounded, values_head)
        return (summed / jnp.transpose(lax.optimization_barrier(jnp.sum(weights, axis=-1)))[:, :, None]).astype(jnp.bfloat16)
    attended = lax.map(attend, jnp.arange(SEQ_BLOCKS, dtype=jnp.int32)).reshape(NEW, QH * HD)
    total = jnp.dot(attended, w_attn_out, preferred_element_type=jnp.float32)
    total = total + jnp.dot(mixed, w_mamba_out, preferred_element_type=jnp.float32)
    layer = (total + hidden_r.astype(jnp.float32)).astype(jnp.bfloat16)
    return (layer, new_flat, states)

def math_sqrt(value):
    return float(value) ** 0.5

def reference(hidden, norm_gain, w_query, w_keyval, w_attn_out, w_inner, w_bc, w_dt, dt_bias, a_log, d_skip, conv_x, conv_bc, mamba_gain, w_mamba_out, cache, cache_len, tail_x, tail_bc, ssm_init):
    layers = []
    keyvals = []
    states = []
    for request in range(REQS):
        layer, new_flat, state_list = one_request(hidden[request], norm_gain, w_query, w_keyval, w_attn_out, w_inner, w_bc, w_dt, dt_bias, a_log, d_skip, conv_x, conv_bc, mamba_gain, w_mamba_out, cache[request], cache_len[request], tail_x[request], tail_bc[request], ssm_init[request])
        layers.append(layer)
        keyvals.append(new_flat)
        states.append(state_list)
    return (jnp.stack(layers), jnp.stack(keyvals), jnp.stack(states))
```

```python
import jax
import jax.numpy as jnp
from jax import lax
from jax.sharding import PartitionSpec as P

HD = 128
QH = 8
KVH = 2
NS = 256
CONV = 4


epsilon = 1e-05
rope_base = 100000000000.0
negative = -1e30


def shifted(block, axis, distance):
    devices = range(lax.axis_size(axis))
    route = [(i - distance, i) for i in devices if i - distance in devices]
    return lax.ppermute(block, axis, route)


def prefix(part, axis, combine, identity):
    place = lax.axis_index(axis)
    gathered = jax.tree.map(lambda a: lax.all_gather(a, axis), part)
    state = jax.tree.map(lambda a, e: jnp.zeros_like(a) + jnp.asarray(e, a.dtype), part, identity)

    def one(turn, state):
        return combine(
            state, jax.tree.map(lambda a: lax.dynamic_index_in_dim(a, turn, 0, False), gathered)
        )

    return lax.fori_loop(0, place, one, state)


def rotate(values, positions):
    half = HD // 2
    freqs = rope_base ** (-jnp.arange(half, dtype=jnp.float32) * 2.0 / HD)
    angles = positions.astype(jnp.float32)[:, None] * freqs[None, :]
    cosine = jnp.cos(angles)[:, None, :]
    sine = jnp.sin(angles)[:, None, :]
    first = values[..., :half]
    second = values[..., half:]
    return jnp.concatenate(
        [first * cosine - second * sine, second * cosine + first * sine], axis=-1
    )


def rms_scale(values):
    mean_sq = jnp.mean(values * values, axis=-1, keepdims=True)
    return values * lax.rsqrt(mean_sq + epsilon)


def causal_conv(tail, inputs, taps):
    padded = jnp.concatenate([tail, inputs], axis=0).astype(jnp.float32)
    count = inputs.shape[0]
    total = jnp.zeros(inputs.shape, jnp.float32)
    for offset in range(CONV):
        total = total + taps[offset].astype(jnp.float32)[None, :] * padded[offset : offset + count]
    return jax.nn.silu(total)


def join_states(earlier, later):
    return (earlier[0] * later[0], later[0][:, None, None] * earlier[1] + later[1])


def shards(
    hidden,
    norm_gain,
    w_query,
    w_keyval,
    w_attn_out,
    w_inner,
    w_bc,
    w_dt,
    dt_bias,
    a_log,
    d_skip,
    conv_x,
    conv_bc,
    mamba_gain,
    w_mamba_out,
    cache,
    cache_len,
    tail_x,
    tail_bc,
    ssm_init,
):
    high = lax.Precision.HIGHEST
    own_rows = hidden[0]
    tokens = own_rows.shape[0]
    seq_pos = lax.axis_index("seq")
    mp_pos = lax.axis_index("mp")
    length = cache_len[0]
    whole = lax.all_gather(own_rows, "mp", axis=1, tiled=True)
    normed = (rms_scale(whole.astype(jnp.float32)) * norm_gain.astype(jnp.float32)).astype(
        jnp.bfloat16
    )
    positions = length + seq_pos * tokens + jnp.arange(tokens, dtype=jnp.int32)
    local_heads = w_query.shape[1] // HD
    query = rotate(
        jnp.dot(normed, w_query, preferred_element_type=jnp.float32).reshape(
            tokens, local_heads, HD
        ),
        positions,
    ).astype(jnp.bfloat16)
    projected = jnp.dot(normed, w_keyval, preferred_element_type=jnp.float32)
    roped = rotate(projected[:, None, :], positions)[:, 0, :]
    kv_block = jnp.where(mp_pos % 2 == 0, roped, projected).astype(jnp.bfloat16)
    bc_block = jnp.dot(normed, w_bc, preferred_element_type=jnp.float32).astype(jnp.bfloat16)
    bc_all = lax.all_gather(bc_block, "mp", axis=1, tiled=True)
    own_rows_kv = jnp.concatenate([cache[0], kv_block], axis=0)
    mp_size = lax.axis_size("mp")
    partner = lax.ppermute(own_rows_kv, "mp", [(i, i ^ 1) for i in range(mp_size)])
    is_key_block = mp_pos % 2 == 0
    group_rows = jnp.where(
        is_key_block,
        jnp.concatenate([own_rows_kv, partner], axis=1),
        jnp.concatenate([partner, own_rows_kv], axis=1),
    )
    inner = jnp.einsum("td,dkc->tkc", normed, w_inner, preferred_element_type=jnp.float32).astype(
        jnp.bfloat16
    )
    rim = CONV - 1
    prev_x, prev_bc = shifted((inner[tokens - rim :, 1], bc_all[tokens - rim :]), "seq", 1)
    first_block = seq_pos == 0
    prev_x = jnp.where(first_block, tail_x[0], prev_x)
    prev_bc = jnp.where(first_block, tail_bc[0], prev_bc)
    mamba_heads = dt_bias.shape[0]
    x_conv = causal_conv(prev_x, inner[:, 1], conv_x).reshape(tokens, mamba_heads, HD)
    bc_conv = causal_conv(prev_bc, bc_all, conv_bc)
    b_mat = bc_conv[:, :NS]
    c_mat = bc_conv[:, NS:]
    step_size = jax.nn.softplus(jnp.dot(normed, w_dt, preferred_element_type=jnp.float32) + dt_bias)
    log_decay = -step_size * jnp.exp(a_log)[None, :]
    cumulative = jnp.cumsum(log_decay, axis=0)
    pairs = jnp.dot(c_mat, b_mat.T, precision=high)
    gap = cumulative[:, None, :] - cumulative[None, :, :]
    token_ids = jnp.arange(tokens)
    lower = (token_ids[:, None] >= token_ids[None, :])[:, :, None]
    decay = jnp.where(lower, jnp.exp(jnp.where(lower, gap, 0.0)), 0.0)
    mixing = decay * pairs[:, :, None] * step_size[None, :, :]
    inner_out = jnp.einsum("tsh,shp->thp", mixing, x_conv, precision=high)
    to_end = jnp.exp(cumulative[-1][None, :] - cumulative) * step_size
    own_state = jnp.einsum("sh,shp,sn->hpn", to_end, x_conv, b_mat, precision=high)
    block_decay = jnp.exp(cumulative[-1])
    scan_decay = block_decay
    scan_state = jnp.where(first_block, block_decay[:, None, None] * ssm_init[0] + own_state, own_state)
    distance = 1
    while distance < lax.axis_size("seq"):
        earlier_decay, earlier_state = shifted((scan_decay, scan_state), "seq", distance)
        reach = seq_pos >= distance
        scan_state = jnp.where(reach, scan_decay[:, None, None] * earlier_state + scan_state, scan_state)
        scan_decay = jnp.where(reach, earlier_decay * scan_decay, scan_decay)
        distance *= 2
    incoming = jnp.where(first_block, ssm_init[0], shifted(scan_state, "seq", 1))
    carried = jnp.exp(cumulative)[:, :, None] * jnp.einsum(
        "tn,hpn->thp", c_mat, incoming, precision=high
    )
    mamba_y = inner_out + carried + d_skip[None, :, None] * x_conv
    state_after = scan_state
    gated = mamba_y * jax.nn.silu(inner[:, 0].astype(jnp.float32).reshape(tokens, mamba_heads, HD))
    mixed = (
        rms_scale(gated).reshape(tokens, mamba_heads * HD) * mamba_gain.astype(jnp.float32)
    ).astype(jnp.bfloat16)
    cache_rows = cache.shape[1]
    shard_rows = cache_rows + tokens
    group = mp_pos * local_heads // (QH // KVH)
    query_index = seq_pos * tokens + jnp.arange(tokens, dtype=jnp.int32)
    scale = 1.0 / float(HD) ** 0.5
    piece = lax.all_gather(group_rows, "seq", axis=0, tiled=True)
    top = jnp.full((local_heads, tokens), negative, jnp.float32)
    count = piece.shape[0]
    index = jnp.arange(count, dtype=jnp.int32)
    owner = index // shard_rows
    offset = index % shard_rows
    in_cache = offset < cache_rows
    slot_ok = in_cache & (owner * cache_rows + offset < length)
    new_index = owner * tokens + offset - cache_rows
    valid = slot_ok[None, :] | (~in_cache)[None, :] & (new_index[None, :] <= query_index[:, None])
    scores = (
        jnp.einsum("qhd,kd->hqk", query, piece[:, :HD], preferred_element_type=jnp.float32) * scale
    )
    masked = jnp.where(valid[None], scores, negative)
    new_top = jnp.maximum(top, jnp.max(masked, axis=-1))
    weights = jnp.where(valid[None], jnp.exp(masked - new_top[:, :, None]), 0.0)
    total = jnp.sum(weights, axis=-1)
    accum = jnp.einsum(
        "hqk,kd->hqd",
        weights.astype(jnp.bfloat16),
        piece[:, HD : 2 * HD],
        preferred_element_type=jnp.float32,
    )
    top, total, accum = (new_top, total, accum)
    attended = jnp.transpose(accum / total[:, :, None], (1, 0, 2)).reshape(tokens, local_heads * HD)
    attended = attended.astype(jnp.bfloat16)
    term = jnp.dot(attended, w_attn_out, preferred_element_type=jnp.float32)
    term = term + jnp.dot(mixed, w_mamba_out, preferred_element_type=jnp.float32)
    summed = lax.psum_scatter(term, "mp", scatter_dimension=1, tiled=True)
    layer = (summed + own_rows.astype(jnp.float32)).astype(jnp.bfloat16)
    return (layer[None], kv_block[None], state_after[None, None])


def solution(mesh):
    placed = (
        P("req", "seq", "mp"),
        P(),
        P(None, "mp"),
        P(None, "mp"),
        P("mp", None),
        P(None, None, "mp"),
        P(None, "mp"),
        P(None, "mp"),
        P("mp"),
        P("mp"),
        P("mp"),
        P(None, "mp"),
        P(),
        P("mp"),
        P("mp", None),
        P("req", "seq", "mp"),
        P("req"),
        P("req", None, "mp"),
        P("req", None, None),
        P("req", "mp", None, None),
    )
    return jax.shard_map(
        shards,
        mesh=mesh,
        in_specs=placed,
        out_specs=(P("req", "seq", "mp"), P("req", "seq", "mp"), P("req", "seq", "mp", None, None)),
        check_vma=False,
    )
```

```python
import jax
import jax.numpy as jnp
from jax import lax
from jax.sharding import PartitionSpec as P

HD = 128
QH = 8
KVH = 2
NS = 256
CONV = 4


epsilon = 1e-05
rope_base = 100000000000.0
negative = -1e30


def shifted(block, axis, distance):
    devices = range(lax.axis_size(axis))
    route = [(i - distance, i) for i in devices if i - distance in devices]
    return lax.ppermute(block, axis, route)


def prefix(part, axis, combine, identity):
    place = lax.axis_index(axis)
    gathered = jax.tree.map(lambda a: lax.all_gather(a, axis), part)
    state = jax.tree.map(lambda a, e: jnp.zeros_like(a) + jnp.asarray(e, a.dtype), part, identity)

    def one(turn, state):
        return combine(
            state, jax.tree.map(lambda a: lax.dynamic_index_in_dim(a, turn, 0, False), gathered)
        )

    return lax.fori_loop(0, place, one, state)


def rotate(values, positions):
    half = HD // 2
    freqs = rope_base ** (-jnp.arange(half, dtype=jnp.float32) * 2.0 / HD)
    angles = positions.astype(jnp.float32)[:, None] * freqs[None, :]
    cosine = jnp.cos(angles)[:, None, :]
    sine = jnp.sin(angles)[:, None, :]
    first = values[..., :half]
    second = values[..., half:]
    return jnp.concatenate(
        [first * cosine - second * sine, second * cosine + first * sine], axis=-1
    )


def rms_scale(values):
    mean_sq = jnp.mean(values * values, axis=-1, keepdims=True)
    return values * lax.rsqrt(mean_sq + epsilon)


def causal_conv(tail, inputs, taps):
    padded = jnp.concatenate([tail, inputs], axis=0).astype(jnp.float32)
    count = inputs.shape[0]
    total = jnp.zeros(inputs.shape, jnp.float32)
    for offset in range(CONV):
        total = total + taps[offset].astype(jnp.float32)[None, :] * padded[offset : offset + count]
    return jax.nn.silu(total)


def join_states(earlier, later):
    return (earlier[0] * later[0], later[0][:, None, None] * earlier[1] + later[1])


def shards(
    hidden,
    norm_gain,
    w_query,
    w_keyval,
    w_attn_out,
    w_inner,
    w_bc,
    w_dt,
    dt_bias,
    a_log,
    d_skip,
    conv_x,
    conv_bc,
    mamba_gain,
    w_mamba_out,
    cache,
    cache_len,
    tail_x,
    tail_bc,
    ssm_init,
):
    high = lax.Precision.HIGHEST
    own_rows = hidden[0]
    tokens = own_rows.shape[0]
    seq_pos = lax.axis_index("seq")
    mp_pos = lax.axis_index("mp")
    length = cache_len[0]
    whole = lax.all_gather(own_rows, "mp", axis=1, tiled=True)
    normed = (rms_scale(whole.astype(jnp.float32)) * norm_gain.astype(jnp.float32)).astype(
        jnp.bfloat16
    )
    positions = length + seq_pos * tokens + jnp.arange(tokens, dtype=jnp.int32)
    local_heads = w_query.shape[1] // HD
    query = rotate(
        jnp.dot(normed, w_query, preferred_element_type=jnp.float32).reshape(
            tokens, local_heads, HD
        ),
        positions,
    ).astype(jnp.bfloat16)
    projected = jnp.dot(normed, w_keyval, preferred_element_type=jnp.float32)
    roped = rotate(projected[:, None, :], positions)[:, 0, :]
    kv_block = jnp.where(mp_pos % 2 == 0, roped, projected).astype(jnp.bfloat16)
    bc_block = jnp.dot(normed, w_bc, preferred_element_type=jnp.float32).astype(jnp.bfloat16)
    bc_all = lax.all_gather(bc_block, "mp", axis=1, tiled=True)
    own_rows_kv = jnp.concatenate([cache[0], kv_block], axis=0)
    mp_size = lax.axis_size("mp")
    partner = lax.ppermute(own_rows_kv, "mp", [(i, i ^ 1) for i in range(mp_size)])
    is_key_block = mp_pos % 2 == 0
    group_rows = jnp.where(
        is_key_block,
        jnp.concatenate([own_rows_kv, partner], axis=1),
        jnp.concatenate([partner, own_rows_kv], axis=1),
    )
    inner = jnp.einsum("td,dkc->tkc", normed, w_inner, preferred_element_type=jnp.float32).astype(
        jnp.bfloat16
    )
    rim = CONV - 1
    prev_x, prev_bc = shifted((inner[tokens - rim :, 1], bc_all[tokens - rim :]), "seq", 1)
    first_block = seq_pos == 0
    prev_x = jnp.where(first_block, tail_x[0], prev_x)
    prev_bc = jnp.where(first_block, tail_bc[0], prev_bc)
    mamba_heads = dt_bias.shape[0]
    x_conv = causal_conv(prev_x, inner[:, 1], conv_x).reshape(tokens, mamba_heads, HD)
    bc_conv = causal_conv(prev_bc, bc_all, conv_bc)
    b_mat = bc_conv[:, :NS]
    c_mat = bc_conv[:, NS:]
    step_size = jax.nn.softplus(jnp.dot(normed, w_dt, preferred_element_type=jnp.float32) + dt_bias)
    log_decay = -step_size * jnp.exp(a_log)[None, :]
    cumulative = jnp.cumsum(log_decay, axis=0)
    pairs = jnp.dot(c_mat, b_mat.T, precision=high)
    gap = cumulative[:, None, :] - cumulative[None, :, :]
    token_ids = jnp.arange(tokens)
    lower = (token_ids[:, None] >= token_ids[None, :])[:, :, None]
    decay = jnp.where(lower, jnp.exp(jnp.where(lower, gap, 0.0)), 0.0)
    mixing = decay * pairs[:, :, None] * step_size[None, :, :]
    inner_out = jnp.einsum("tsh,shp->thp", mixing, x_conv, precision=high)
    to_end = jnp.exp(cumulative[-1][None, :] - cumulative) * step_size
    own_state = jnp.einsum("sh,shp,sn->hpn", to_end, x_conv, b_mat, precision=high)
    block_decay = jnp.exp(cumulative[-1])
    seq_size = lax.axis_size("seq")
    rows = HD // seq_size
    pieces = jnp.transpose(own_state.reshape(mamba_heads, seq_size, rows, NS), (1, 0, 2, 3))
    decays = jnp.broadcast_to(block_decay[None, :, None, None], (seq_size, mamba_heads, 1, NS))
    columns = lax.all_to_all(jnp.concatenate([pieces, decays], axis=2), "seq", 0, 0, tiled=True)
    carry = lax.dynamic_slice_in_dim(ssm_init[0], seq_pos * rows, rows, 1)
    entering = []
    for source in range(seq_size):
        entering.append(carry)
        part = columns[source]
        carry = part[:, rows:, :] * carry + part[:, :rows, :]
    entering = lax.all_to_all(jnp.stack(entering, axis=0), "seq", 0, 0, tiled=True)
    incoming = jnp.transpose(entering, (1, 0, 2, 3)).reshape(mamba_heads, HD, NS)
    carried = jnp.exp(cumulative)[:, :, None] * jnp.einsum(
        "tn,hpn->thp", c_mat, incoming, precision=high
    )
    mamba_y = inner_out + carried + d_skip[None, :, None] * x_conv
    state_after = block_decay[:, None, None] * incoming + own_state
    gated = mamba_y * jax.nn.silu(inner[:, 0].astype(jnp.float32).reshape(tokens, mamba_heads, HD))
    mixed = (
        rms_scale(gated).reshape(tokens, mamba_heads * HD) * mamba_gain.astype(jnp.float32)
    ).astype(jnp.bfloat16)
    cache_rows = cache.shape[1]
    shard_rows = cache_rows + tokens
    group = mp_pos * local_heads // (QH // KVH)
    query_index = seq_pos * tokens + jnp.arange(tokens, dtype=jnp.int32)
    scale = 1.0 / float(HD) ** 0.5
    piece = lax.all_gather(group_rows, "seq", axis=0, tiled=True)
    top = jnp.full((local_heads, tokens), negative, jnp.float32)
    count = piece.shape[0]
    index = jnp.arange(count, dtype=jnp.int32)
    owner = index // shard_rows
    offset = index % shard_rows
    in_cache = offset < cache_rows
    slot_ok = in_cache & (owner * cache_rows + offset < length)
    new_index = owner * tokens + offset - cache_rows
    valid = slot_ok[None, :] | (~in_cache)[None, :] & (new_index[None, :] <= query_index[:, None])
    scores = (
        jnp.einsum("qhd,kd->hqk", query, piece[:, :HD], preferred_element_type=jnp.float32) * scale
    )
    masked = jnp.where(valid[None], scores, negative)
    new_top = jnp.maximum(top, jnp.max(masked, axis=-1))
    weights = jnp.where(valid[None], jnp.exp(masked - new_top[:, :, None]), 0.0)
    total = jnp.sum(weights, axis=-1)
    accum = jnp.einsum(
        "hqk,kd->hqd",
        weights.astype(jnp.bfloat16),
        piece[:, HD : 2 * HD],
        preferred_element_type=jnp.float32,
    )
    top, total, accum = (new_top, total, accum)
    attended = jnp.transpose(accum / total[:, :, None], (1, 0, 2)).reshape(tokens, local_heads * HD)
    attended = attended.astype(jnp.bfloat16)
    term = jnp.dot(attended, w_attn_out, preferred_element_type=jnp.float32)
    term = term + jnp.dot(mixed, w_mamba_out, preferred_element_type=jnp.float32)
    summed = lax.psum_scatter(term, "mp", scatter_dimension=1, tiled=True)
    layer = (summed + own_rows.astype(jnp.float32)).astype(jnp.bfloat16)
    return (layer[None], kv_block[None], state_after[None, None])


def solution(mesh):
    placed = (
        P("req", "seq", "mp"),
        P(),
        P(None, "mp"),
        P(None, "mp"),
        P("mp", None),
        P(None, None, "mp"),
        P(None, "mp"),
        P(None, "mp"),
        P("mp"),
        P("mp"),
        P("mp"),
        P(None, "mp"),
        P(),
        P("mp"),
        P("mp", None),
        P("req", "seq", "mp"),
        P("req"),
        P("req", None, "mp"),
        P("req", None, None),
        P("req", "mp", None, None),
    )
    return jax.shard_map(
        shards,
        mesh=mesh,
        in_specs=placed,
        out_specs=(P("req", "seq", "mp"), P("req", "seq", "mp"), P("req", "seq", "mp", None, None)),
        check_vma=False,
    )
```

```python
import jax
import jax.numpy as jnp
from jax import lax
from jax.sharding import PartitionSpec as P

HD = 128
QH = 8
KVH = 2
NS = 256
CONV = 4


epsilon = 1e-05
rope_base = 100000000000.0
negative = -1e30


def shifted(block, axis, distance):
    devices = range(lax.axis_size(axis))
    route = [(i - distance, i) for i in devices if i - distance in devices]
    return lax.ppermute(block, axis, route)


def prefix(part, axis, combine, identity):
    place = lax.axis_index(axis)
    gathered = jax.tree.map(lambda a: lax.all_gather(a, axis), part)
    state = jax.tree.map(lambda a, e: jnp.zeros_like(a) + jnp.asarray(e, a.dtype), part, identity)

    def one(turn, state):
        return combine(
            state, jax.tree.map(lambda a: lax.dynamic_index_in_dim(a, turn, 0, False), gathered)
        )

    return lax.fori_loop(0, place, one, state)


def rotate(values, positions):
    half = HD // 2
    freqs = rope_base ** (-jnp.arange(half, dtype=jnp.float32) * 2.0 / HD)
    angles = positions.astype(jnp.float32)[:, None] * freqs[None, :]
    cosine = jnp.cos(angles)[:, None, :]
    sine = jnp.sin(angles)[:, None, :]
    first = values[..., :half]
    second = values[..., half:]
    return jnp.concatenate(
        [first * cosine - second * sine, second * cosine + first * sine], axis=-1
    )


def rms_scale(values):
    mean_sq = jnp.mean(values * values, axis=-1, keepdims=True)
    return values * lax.rsqrt(mean_sq + epsilon)


def causal_conv(tail, inputs, taps):
    padded = jnp.concatenate([tail, inputs], axis=0).astype(jnp.float32)
    count = inputs.shape[0]
    total = jnp.zeros(inputs.shape, jnp.float32)
    for offset in range(CONV):
        total = total + taps[offset].astype(jnp.float32)[None, :] * padded[offset : offset + count]
    return jax.nn.silu(total)


def join_states(earlier, later):
    return (earlier[0] * later[0], later[0][:, None, None] * earlier[1] + later[1])


def shards(
    hidden,
    norm_gain,
    w_query,
    w_keyval,
    w_attn_out,
    w_inner,
    w_bc,
    w_dt,
    dt_bias,
    a_log,
    d_skip,
    conv_x,
    conv_bc,
    mamba_gain,
    w_mamba_out,
    cache,
    cache_len,
    tail_x,
    tail_bc,
    ssm_init,
):
    high = lax.Precision.HIGHEST
    own_rows = hidden[0]
    tokens = own_rows.shape[0]
    seq_pos = lax.axis_index("seq")
    mp_pos = lax.axis_index("mp")
    length = cache_len[0]
    whole = lax.all_gather(own_rows, "mp", axis=1, tiled=True)
    normed = (rms_scale(whole.astype(jnp.float32)) * norm_gain.astype(jnp.float32)).astype(
        jnp.bfloat16
    )
    positions = length + seq_pos * tokens + jnp.arange(tokens, dtype=jnp.int32)
    local_heads = w_query.shape[1] // HD
    query = rotate(
        jnp.dot(normed, w_query, preferred_element_type=jnp.float32).reshape(
            tokens, local_heads, HD
        ),
        positions,
    ).astype(jnp.bfloat16)
    projected = jnp.dot(normed, w_keyval, preferred_element_type=jnp.float32)
    roped = rotate(projected[:, None, :], positions)[:, 0, :]
    kv_block = jnp.where(mp_pos % 2 == 0, roped, projected).astype(jnp.bfloat16)
    bc_block = jnp.dot(normed, w_bc, preferred_element_type=jnp.float32).astype(jnp.bfloat16)
    bc_all = lax.all_gather(bc_block, "mp", axis=1, tiled=True)
    mp_size = lax.axis_size("mp")
    pairs_of = [(i, i ^ 1) for i in range(mp_size)]
    is_key_block = mp_pos % 2 == 0

    def paired(own):
        other = lax.ppermute(own, "mp", pairs_of)
        return jnp.where(
            is_key_block,
            jnp.concatenate([own, other], axis=1),
            jnp.concatenate([other, own], axis=1),
        )

    cache_all = lax.all_gather(paired(cache[0]), "seq", axis=0, tiled=True)
    new_all = lax.all_gather(paired(kv_block), "seq", axis=0, tiled=True)
    inner = jnp.einsum("td,dkc->tkc", normed, w_inner, preferred_element_type=jnp.float32).astype(
        jnp.bfloat16
    )
    rim = CONV - 1
    prev_x, prev_bc = shifted((inner[tokens - rim :, 1], bc_all[tokens - rim :]), "seq", 1)
    first_block = seq_pos == 0
    prev_x = jnp.where(first_block, tail_x[0], prev_x)
    prev_bc = jnp.where(first_block, tail_bc[0], prev_bc)
    mamba_heads = dt_bias.shape[0]
    x_conv = causal_conv(prev_x, inner[:, 1], conv_x).reshape(tokens, mamba_heads, HD)
    bc_conv = causal_conv(prev_bc, bc_all, conv_bc)
    b_mat = bc_conv[:, :NS]
    c_mat = bc_conv[:, NS:]
    step_size = jax.nn.softplus(jnp.dot(normed, w_dt, preferred_element_type=jnp.float32) + dt_bias)
    log_decay = -step_size * jnp.exp(a_log)[None, :]
    cumulative = jnp.cumsum(log_decay, axis=0)
    pairs = jnp.dot(c_mat, b_mat.T, precision=high)
    gap = cumulative[:, None, :] - cumulative[None, :, :]
    token_ids = jnp.arange(tokens)
    lower = (token_ids[:, None] >= token_ids[None, :])[:, :, None]
    decay = jnp.where(lower, jnp.exp(jnp.where(lower, gap, 0.0)), 0.0)
    mixing = decay * pairs[:, :, None] * step_size[None, :, :]
    inner_out = jnp.einsum("tsh,shp->thp", mixing, x_conv, precision=high)
    to_end = jnp.exp(cumulative[-1][None, :] - cumulative) * step_size
    own_state = jnp.einsum("sh,shp,sn->hpn", to_end, x_conv, b_mat, precision=high)
    block_decay = jnp.exp(cumulative[-1])
    seq_size = lax.axis_size("seq")
    rows = HD // seq_size
    pieces = jnp.transpose(own_state.reshape(mamba_heads, seq_size, rows, NS), (1, 0, 2, 3))
    decays = jnp.broadcast_to(block_decay[None, :, None, None], (seq_size, mamba_heads, 1, NS))
    columns = lax.all_to_all(jnp.concatenate([pieces, decays], axis=2), "seq", 0, 0, tiled=True)
    carry = lax.dynamic_slice_in_dim(ssm_init[0], seq_pos * rows, rows, 1)
    entering = []
    for source in range(seq_size):
        entering.append(carry)
        part = columns[source]
        carry = part[:, rows:, :] * carry + part[:, :rows, :]
    entering = lax.all_to_all(jnp.stack(entering, axis=0), "seq", 0, 0, tiled=True)
    incoming = jnp.transpose(entering, (1, 0, 2, 3)).reshape(mamba_heads, HD, NS)
    carried = jnp.exp(cumulative)[:, :, None] * jnp.einsum(
        "tn,hpn->thp", c_mat, incoming, precision=high
    )
    mamba_y = inner_out + carried + d_skip[None, :, None] * x_conv
    state_after = block_decay[:, None, None] * incoming + own_state
    gated = mamba_y * jax.nn.silu(inner[:, 0].astype(jnp.float32).reshape(tokens, mamba_heads, HD))
    mixed = (
        rms_scale(gated).reshape(tokens, mamba_heads * HD) * mamba_gain.astype(jnp.float32)
    ).astype(jnp.bfloat16)
    cache_rows = cache.shape[1]
    shard_rows = cache_rows + tokens
    group = mp_pos * local_heads // (QH // KVH)
    query_index = seq_pos * tokens + jnp.arange(tokens, dtype=jnp.int32)
    scale = 1.0 / float(HD) ** 0.5
    piece = jnp.concatenate([cache_all, new_all], axis=0)
    top = jnp.full((local_heads, tokens), negative, jnp.float32)
    total_cache = cache_all.shape[0]
    index = jnp.arange(piece.shape[0], dtype=jnp.int32)
    in_cache = index < total_cache
    slot_ok = in_cache & (index < length)
    new_index = index - total_cache
    valid = slot_ok[None, :] | (~in_cache)[None, :] & (new_index[None, :] <= query_index[:, None])
    scores = (
        jnp.einsum("qhd,kd->hqk", query, piece[:, :HD], preferred_element_type=jnp.float32) * scale
    )
    masked = jnp.where(valid[None], scores, negative)
    new_top = jnp.maximum(top, jnp.max(masked, axis=-1))
    weights = jnp.where(valid[None], jnp.exp(masked - new_top[:, :, None]), 0.0)
    total = jnp.sum(weights, axis=-1)
    accum = jnp.einsum(
        "hqk,kd->hqd",
        weights.astype(jnp.bfloat16),
        piece[:, HD : 2 * HD],
        preferred_element_type=jnp.float32,
    )
    top, total, accum = (new_top, total, accum)
    attended = jnp.transpose(accum / total[:, :, None], (1, 0, 2)).reshape(tokens, local_heads * HD)
    attended = attended.astype(jnp.bfloat16)
    term = jnp.dot(attended, w_attn_out, preferred_element_type=jnp.float32)
    term = term + jnp.dot(mixed, w_mamba_out, preferred_element_type=jnp.float32)
    summed = lax.psum_scatter(term, "mp", scatter_dimension=1, tiled=True)
    layer = (summed + own_rows.astype(jnp.float32)).astype(jnp.bfloat16)
    return (layer[None], kv_block[None], state_after[None, None])


def solution(mesh):
    placed = (
        P("req", "seq", "mp"),
        P(),
        P(None, "mp"),
        P(None, "mp"),
        P("mp", None),
        P(None, None, "mp"),
        P(None, "mp"),
        P(None, "mp"),
        P("mp"),
        P("mp"),
        P("mp"),
        P(None, "mp"),
        P(),
        P("mp"),
        P("mp", None),
        P("req", "seq", "mp"),
        P("req"),
        P("req", None, "mp"),
        P("req", None, None),
        P("req", "mp", None, None),
    )
    return jax.shard_map(
        shards,
        mesh=mesh,
        in_specs=placed,
        out_specs=(P("req", "seq", "mp"), P("req", "seq", "mp"), P("req", "seq", "mp", None, None)),
        check_vma=False,
    )
```

```python
import jax
import jax.numpy as jnp
from jax import lax
from jax.sharding import PartitionSpec as P
from jax.experimental import pallas as pl
from jax.experimental.pallas import tpu as pltpu

HD = 128
QH = 8
KVH = 2
NS = 256
CONV = 4


epsilon = 1e-05
rope_base = 100000000000.0
negative = -1e30


def shifted(block, axis, distance):
    devices = range(lax.axis_size(axis))
    route = [(i - distance, i) for i in devices if i - distance in devices]
    return lax.ppermute(block, axis, route)


def prefix(part, axis, combine, identity):
    place = lax.axis_index(axis)
    gathered = jax.tree.map(lambda a: lax.all_gather(a, axis), part)
    state = jax.tree.map(lambda a, e: jnp.zeros_like(a) + jnp.asarray(e, a.dtype), part, identity)

    def one(turn, state):
        return combine(
            state, jax.tree.map(lambda a: lax.dynamic_index_in_dim(a, turn, 0, False), gathered)
        )

    return lax.fori_loop(0, place, one, state)


def gather_rows(block, axis, tag):
    count = lax.axis_size(axis)
    rows = block.shape[0]
    mesh_id = pl.DeviceIdType.MESH

    def where_is(place):
        return (place, lax.axis_index("mp"), lax.axis_index("req"))

    def kernel(x_ref, out_ref, local_sem, send_sem, recv_sem):
        me = lax.axis_index(axis)
        barrier = pltpu.get_barrier_semaphore()

        def greet(step, carry):
            pl.semaphore_signal(
                barrier, inc=1, device_id=where_is(lax.rem(me + step, count)), device_id_type=mesh_id
            )
            return carry

        lax.fori_loop(1, count, greet, 0)
        pl.semaphore_wait(barrier, count - 1)
        own = pltpu.make_async_copy(x_ref, out_ref.at[pl.ds(me * rows, rows)], local_sem)
        own.start()

        def remote(step, source, target):
            return pltpu.make_async_remote_copy(
                src_ref=x_ref,
                dst_ref=out_ref.at[pl.ds(source * rows, rows)],
                send_sem=send_sem.at[step],
                recv_sem=recv_sem.at[step],
                device_id=where_is(target),
                device_id_type=mesh_id,
            )

        def send(step, carry):
            remote(step, me, lax.rem(me + step, count)).start()
            return carry

        lax.fori_loop(1, count, send, 0)

        def finish(step, carry):
            remote(step, me, lax.rem(me + step, count)).wait_send()
            source = lax.rem(me + count - step, count)
            remote(step, source, source).wait_recv()
            return carry

        lax.fori_loop(1, count, finish, 0)
        own.wait()

    return pl.pallas_call(
        kernel,
        out_shape=jax.ShapeDtypeStruct((count * rows,) + block.shape[1:], block.dtype),
        in_specs=[pl.BlockSpec(memory_space=pl.ANY)],
        out_specs=pl.BlockSpec(memory_space=pl.ANY),
        scratch_shapes=[
            pltpu.SemaphoreType.DMA(()),
            pltpu.SemaphoreType.DMA((count,)),
            pltpu.SemaphoreType.DMA((count,)),
        ],
        compiler_params=pltpu.CompilerParams(collective_id=tag, has_side_effects=True),
    )(block)


def rotate(values, positions):
    half = HD // 2
    freqs = rope_base ** (-jnp.arange(half, dtype=jnp.float32) * 2.0 / HD)
    angles = positions.astype(jnp.float32)[:, None] * freqs[None, :]
    cosine = jnp.cos(angles)[:, None, :]
    sine = jnp.sin(angles)[:, None, :]
    first = values[..., :half]
    second = values[..., half:]
    return jnp.concatenate(
        [first * cosine - second * sine, second * cosine + first * sine], axis=-1
    )


def rms_scale(values):
    mean_sq = jnp.mean(values * values, axis=-1, keepdims=True)
    return values * lax.rsqrt(mean_sq + epsilon)


def causal_conv(tail, inputs, taps):
    padded = jnp.concatenate([tail, inputs], axis=0).astype(jnp.float32)
    count = inputs.shape[0]
    total = jnp.zeros(inputs.shape, jnp.float32)
    for offset in range(CONV):
        total = total + taps[offset].astype(jnp.float32)[None, :] * padded[offset : offset + count]
    return jax.nn.silu(total)


def join_states(earlier, later):
    return (earlier[0] * later[0], later[0][:, None, None] * earlier[1] + later[1])


def shards(
    hidden,
    norm_gain,
    w_query,
    w_keyval,
    w_attn_out,
    w_inner,
    w_bc,
    w_dt,
    dt_bias,
    a_log,
    d_skip,
    conv_x,
    conv_bc,
    mamba_gain,
    w_mamba_out,
    cache,
    cache_len,
    tail_x,
    tail_bc,
    ssm_init,
):
    high = lax.Precision.HIGHEST
    own_rows = hidden[0]
    tokens = own_rows.shape[0]
    seq_pos = lax.axis_index("seq")
    mp_pos = lax.axis_index("mp")
    length = cache_len[0]
    whole = lax.all_gather(own_rows, "mp", axis=1, tiled=True)
    normed = (rms_scale(whole.astype(jnp.float32)) * norm_gain.astype(jnp.float32)).astype(
        jnp.bfloat16
    )
    positions = length + seq_pos * tokens + jnp.arange(tokens, dtype=jnp.int32)
    local_heads = w_query.shape[1] // HD
    query = rotate(
        jnp.dot(normed, w_query, preferred_element_type=jnp.float32).reshape(
            tokens, local_heads, HD
        ),
        positions,
    ).astype(jnp.bfloat16)
    projected = jnp.dot(normed, w_keyval, preferred_element_type=jnp.float32)
    roped = rotate(projected[:, None, :], positions)[:, 0, :]
    kv_block = jnp.where(mp_pos % 2 == 0, roped, projected).astype(jnp.bfloat16)
    bc_block = jnp.dot(normed, w_bc, preferred_element_type=jnp.float32).astype(jnp.bfloat16)
    bc_all = lax.all_gather(bc_block, "mp", axis=1, tiled=True)
    mp_size = lax.axis_size("mp")
    pairs_of = [(i, i ^ 1) for i in range(mp_size)]
    is_key_block = mp_pos % 2 == 0

    def paired(own):
        other = lax.ppermute(own, "mp", pairs_of)
        return jnp.where(
            is_key_block,
            jnp.concatenate([own, other], axis=1),
            jnp.concatenate([other, own], axis=1),
        )

    cache_all = gather_rows(paired(cache[0]), "seq", 0)
    new_all = gather_rows(paired(kv_block), "seq", 1)
    inner = jnp.einsum("td,dkc->tkc", normed, w_inner, preferred_element_type=jnp.float32).astype(
        jnp.bfloat16
    )
    rim = CONV - 1
    prev_x, prev_bc = shifted((inner[tokens - rim :, 1], bc_all[tokens - rim :]), "seq", 1)
    first_block = seq_pos == 0
    prev_x = jnp.where(first_block, tail_x[0], prev_x)
    prev_bc = jnp.where(first_block, tail_bc[0], prev_bc)
    mamba_heads = dt_bias.shape[0]
    x_conv = causal_conv(prev_x, inner[:, 1], conv_x).reshape(tokens, mamba_heads, HD)
    bc_conv = causal_conv(prev_bc, bc_all, conv_bc)
    b_mat = bc_conv[:, :NS]
    c_mat = bc_conv[:, NS:]
    step_size = jax.nn.softplus(jnp.dot(normed, w_dt, preferred_element_type=jnp.float32) + dt_bias)
    log_decay = -step_size * jnp.exp(a_log)[None, :]
    cumulative = jnp.cumsum(log_decay, axis=0)
    pairs = jnp.dot(c_mat, b_mat.T, precision=high)
    gap = cumulative[:, None, :] - cumulative[None, :, :]
    token_ids = jnp.arange(tokens)
    lower = (token_ids[:, None] >= token_ids[None, :])[:, :, None]
    decay = jnp.where(lower, jnp.exp(jnp.where(lower, gap, 0.0)), 0.0)
    mixing = decay * pairs[:, :, None] * step_size[None, :, :]
    inner_out = jnp.einsum("tsh,shp->thp", mixing, x_conv, precision=high)
    to_end = jnp.exp(cumulative[-1][None, :] - cumulative) * step_size
    own_state = jnp.einsum("sh,shp,sn->hpn", to_end, x_conv, b_mat, precision=high)
    block_decay = jnp.exp(cumulative[-1])
    seq_size = lax.axis_size("seq")
    rows = HD // seq_size
    pieces = jnp.transpose(own_state.reshape(mamba_heads, seq_size, rows, NS), (1, 0, 2, 3))
    decays = jnp.broadcast_to(block_decay[None, :, None, None], (seq_size, mamba_heads, 1, NS))
    columns = lax.all_to_all(jnp.concatenate([pieces, decays], axis=2), "seq", 0, 0, tiled=True)
    carry = lax.dynamic_slice_in_dim(ssm_init[0], seq_pos * rows, rows, 1)
    entering = []
    for source in range(seq_size):
        entering.append(carry)
        part = columns[source]
        carry = part[:, rows:, :] * carry + part[:, :rows, :]
    entering = lax.all_to_all(jnp.stack(entering, axis=0), "seq", 0, 0, tiled=True)
    incoming = jnp.transpose(entering, (1, 0, 2, 3)).reshape(mamba_heads, HD, NS)
    carried = jnp.exp(cumulative)[:, :, None] * jnp.einsum(
        "tn,hpn->thp", c_mat, incoming, precision=high
    )
    mamba_y = inner_out + carried + d_skip[None, :, None] * x_conv
    state_after = block_decay[:, None, None] * incoming + own_state
    gated = mamba_y * jax.nn.silu(inner[:, 0].astype(jnp.float32).reshape(tokens, mamba_heads, HD))
    mixed = (
        rms_scale(gated).reshape(tokens, mamba_heads * HD) * mamba_gain.astype(jnp.float32)
    ).astype(jnp.bfloat16)
    cache_rows = cache.shape[1]
    shard_rows = cache_rows + tokens
    group = mp_pos * local_heads // (QH // KVH)
    query_index = seq_pos * tokens + jnp.arange(tokens, dtype=jnp.int32)
    scale = 1.0 / float(HD) ** 0.5
    piece = jnp.concatenate([cache_all, new_all], axis=0)
    top = jnp.full((local_heads, tokens), negative, jnp.float32)
    total_cache = cache_all.shape[0]
    index = jnp.arange(piece.shape[0], dtype=jnp.int32)
    in_cache = index < total_cache
    slot_ok = in_cache & (index < length)
    new_index = index - total_cache
    valid = slot_ok[None, :] | (~in_cache)[None, :] & (new_index[None, :] <= query_index[:, None])
    scores = (
        jnp.einsum("qhd,kd->hqk", query, piece[:, :HD], preferred_element_type=jnp.float32) * scale
    )
    masked = jnp.where(valid[None], scores, negative)
    new_top = jnp.maximum(top, jnp.max(masked, axis=-1))
    weights = jnp.where(valid[None], jnp.exp(masked - new_top[:, :, None]), 0.0)
    total = jnp.sum(weights, axis=-1)
    accum = jnp.einsum(
        "hqk,kd->hqd",
        weights.astype(jnp.bfloat16),
        piece[:, HD : 2 * HD],
        preferred_element_type=jnp.float32,
    )
    top, total, accum = (new_top, total, accum)
    attended = jnp.transpose(accum / total[:, :, None], (1, 0, 2)).reshape(tokens, local_heads * HD)
    attended = attended.astype(jnp.bfloat16)
    term = jnp.dot(attended, w_attn_out, preferred_element_type=jnp.float32)
    term = term + jnp.dot(mixed, w_mamba_out, preferred_element_type=jnp.float32)
    summed = lax.psum_scatter(term, "mp", scatter_dimension=1, tiled=True)
    layer = (summed + own_rows.astype(jnp.float32)).astype(jnp.bfloat16)
    return (layer[None], kv_block[None], state_after[None, None])


def solution(mesh):
    placed = (
        P("req", "seq", "mp"),
        P(),
        P(None, "mp"),
        P(None, "mp"),
        P("mp", None),
        P(None, None, "mp"),
        P(None, "mp"),
        P(None, "mp"),
        P("mp"),
        P("mp"),
        P("mp"),
        P(None, "mp"),
        P(),
        P("mp"),
        P("mp", None),
        P("req", "seq", "mp"),
        P("req"),
        P("req", None, "mp"),
        P("req", None, None),
        P("req", "mp", None, None),
    )
    return jax.shard_map(
        shards,
        mesh=mesh,
        in_specs=placed,
        out_specs=(P("req", "seq", "mp"), P("req", "seq", "mp"), P("req", "seq", "mp", None, None)),
        check_vma=False,
    )
```

```python
import jax
import jax.numpy as jnp
from jax import lax
from jax.sharding import PartitionSpec as P
from jax.experimental import pallas as pl
from jax.experimental.pallas import tpu as pltpu

HD = 128
QH = 8
KVH = 2
NS = 256
CONV = 4


epsilon = 1e-05
rope_base = 100000000000.0
negative = -1e30


def shifted(block, axis, distance):
    devices = range(lax.axis_size(axis))
    route = [(i - distance, i) for i in devices if i - distance in devices]
    return lax.ppermute(block, axis, route)


def prefix(part, axis, combine, identity):
    place = lax.axis_index(axis)
    gathered = jax.tree.map(lambda a: lax.all_gather(a, axis), part)
    state = jax.tree.map(lambda a, e: jnp.zeros_like(a) + jnp.asarray(e, a.dtype), part, identity)

    def one(turn, state):
        return combine(
            state, jax.tree.map(lambda a: lax.dynamic_index_in_dim(a, turn, 0, False), gathered)
        )

    return lax.fori_loop(0, place, one, state)


def attend(query_rows, query_rank, pieces, key_rank, block):
    rows = query_rows.shape[0]
    count = pieces.shape[0]
    steps = count // block
    scale = 1.0 / float(HD) ** 0.5

    def kernel(qr_ref, q_ref, kr_ref, kv_ref, out_ref, top_ref, total_ref, acc_ref):
        step = pl.program_id(0)

        @pl.when(step == 0)
        def _():
            top_ref[...] = jnp.full(top_ref.shape, negative, jnp.float32)
            total_ref[...] = jnp.zeros(total_ref.shape, jnp.float32)
            acc_ref[...] = jnp.zeros(acc_ref.shape, jnp.float32)

        scores = lax.dot_general(
            q_ref[...], kv_ref[:, :HD], (((1,), (1,)), ((), ())), preferred_element_type=jnp.float32
        ) * scale
        valid = kr_ref[...] <= qr_ref[...]
        masked = jnp.where(valid, scores, negative)
        old = top_ref[...]
        new = jnp.maximum(old, jnp.max(masked, axis=1, keepdims=True))
        weights = jnp.where(valid, jnp.exp(masked - new), 0.0)
        alpha = jnp.exp(old - new)
        total_ref[...] = alpha * total_ref[...] + jnp.sum(weights, axis=1, keepdims=True)
        acc_ref[...] = alpha * acc_ref[...] + jnp.dot(
            weights.astype(jnp.bfloat16), kv_ref[:, HD:], preferred_element_type=jnp.float32
        )
        top_ref[...] = new

        @pl.when(step == steps - 1)
        def _():
            out_ref[...] = (acc_ref[...] / total_ref[...]).astype(out_ref.dtype)

    return pl.pallas_call(
        kernel,
        grid=(steps,),
        in_specs=[
            pl.BlockSpec((rows, 1), lambda i: (0, 0)),
            pl.BlockSpec((rows, HD), lambda i: (0, 0)),
            pl.BlockSpec((1, block), lambda i: (0, i)),
            pl.BlockSpec((block, 2 * HD), lambda i: (i, 0)),
        ],
        out_specs=pl.BlockSpec((rows, HD), lambda i: (0, 0)),
        out_shape=jax.ShapeDtypeStruct((rows, HD), jnp.bfloat16),
        scratch_shapes=[
            pltpu.VMEM((rows, 1), jnp.float32),
            pltpu.VMEM((rows, 1), jnp.float32),
            pltpu.VMEM((rows, HD), jnp.float32),
        ],
        compiler_params=pltpu.CompilerParams(vmem_limit_bytes=48 * 1024 * 1024),
    )(query_rank, query_rows, key_rank, pieces)


def rotate(values, positions):
    half = HD // 2
    freqs = rope_base ** (-jnp.arange(half, dtype=jnp.float32) * 2.0 / HD)
    angles = positions.astype(jnp.float32)[:, None] * freqs[None, :]
    cosine = jnp.cos(angles)[:, None, :]
    sine = jnp.sin(angles)[:, None, :]
    first = values[..., :half]
    second = values[..., half:]
    return jnp.concatenate(
        [first * cosine - second * sine, second * cosine + first * sine], axis=-1
    )


def rms_scale(values):
    mean_sq = jnp.mean(values * values, axis=-1, keepdims=True)
    return values * lax.rsqrt(mean_sq + epsilon)


def causal_conv(tail, inputs, taps):
    padded = jnp.concatenate([tail, inputs], axis=0).astype(jnp.float32)
    count = inputs.shape[0]
    total = jnp.zeros(inputs.shape, jnp.float32)
    for offset in range(CONV):
        total = total + taps[offset].astype(jnp.float32)[None, :] * padded[offset : offset + count]
    return jax.nn.silu(total)


def join_states(earlier, later):
    return (earlier[0] * later[0], later[0][:, None, None] * earlier[1] + later[1])


def shards(
    hidden,
    norm_gain,
    w_query,
    w_keyval,
    w_attn_out,
    w_inner,
    w_bc,
    w_dt,
    dt_bias,
    a_log,
    d_skip,
    conv_x,
    conv_bc,
    mamba_gain,
    w_mamba_out,
    cache,
    cache_len,
    tail_x,
    tail_bc,
    ssm_init,
):
    high = lax.Precision.HIGHEST
    own_rows = hidden[0]
    tokens = own_rows.shape[0]
    seq_pos = lax.axis_index("seq")
    mp_pos = lax.axis_index("mp")
    length = cache_len[0]
    whole = lax.all_gather(own_rows, "mp", axis=1, tiled=True)
    normed = (rms_scale(whole.astype(jnp.float32)) * norm_gain.astype(jnp.float32)).astype(
        jnp.bfloat16
    )
    positions = length + seq_pos * tokens + jnp.arange(tokens, dtype=jnp.int32)
    local_heads = w_query.shape[1] // HD
    query = rotate(
        jnp.dot(normed, w_query, preferred_element_type=jnp.float32).reshape(
            tokens, local_heads, HD
        ),
        positions,
    ).astype(jnp.bfloat16)
    projected = jnp.dot(normed, w_keyval, preferred_element_type=jnp.float32)
    roped = rotate(projected[:, None, :], positions)[:, 0, :]
    kv_block = jnp.where(mp_pos % 2 == 0, roped, projected).astype(jnp.bfloat16)
    bc_block = jnp.dot(normed, w_bc, preferred_element_type=jnp.float32).astype(jnp.bfloat16)
    bc_all = lax.all_gather(bc_block, "mp", axis=1, tiled=True)
    own_rows_kv = jnp.concatenate([cache[0], kv_block], axis=0)
    mp_size = lax.axis_size("mp")
    partner = lax.ppermute(own_rows_kv, "mp", [(i, i ^ 1) for i in range(mp_size)])
    is_key_block = mp_pos % 2 == 0
    group_rows = jnp.where(
        is_key_block,
        jnp.concatenate([own_rows_kv, partner], axis=1),
        jnp.concatenate([partner, own_rows_kv], axis=1),
    )
    inner = jnp.einsum("td,dkc->tkc", normed, w_inner, preferred_element_type=jnp.float32).astype(
        jnp.bfloat16
    )
    rim = CONV - 1
    prev_x, prev_bc = shifted((inner[tokens - rim :, 1], bc_all[tokens - rim :]), "seq", 1)
    first_block = seq_pos == 0
    prev_x = jnp.where(first_block, tail_x[0], prev_x)
    prev_bc = jnp.where(first_block, tail_bc[0], prev_bc)
    mamba_heads = dt_bias.shape[0]
    x_conv = causal_conv(prev_x, inner[:, 1], conv_x).reshape(tokens, mamba_heads, HD)
    bc_conv = causal_conv(prev_bc, bc_all, conv_bc)
    b_mat = bc_conv[:, :NS]
    c_mat = bc_conv[:, NS:]
    step_size = jax.nn.softplus(jnp.dot(normed, w_dt, preferred_element_type=jnp.float32) + dt_bias)
    log_decay = -step_size * jnp.exp(a_log)[None, :]
    cumulative = jnp.cumsum(log_decay, axis=0)
    pairs = jnp.dot(c_mat, b_mat.T, precision=high)
    gap = cumulative[:, None, :] - cumulative[None, :, :]
    token_ids = jnp.arange(tokens)
    lower = (token_ids[:, None] >= token_ids[None, :])[:, :, None]
    decay = jnp.where(lower, jnp.exp(jnp.where(lower, gap, 0.0)), 0.0)
    mixing = decay * pairs[:, :, None] * step_size[None, :, :]
    inner_out = jnp.einsum("tsh,shp->thp", mixing, x_conv, precision=high)
    to_end = jnp.exp(cumulative[-1][None, :] - cumulative) * step_size
    own_state = jnp.einsum("sh,shp,sn->hpn", to_end, x_conv, b_mat, precision=high)
    block_decay = jnp.exp(cumulative[-1])
    seq_size = lax.axis_size("seq")
    rows = HD // seq_size
    pieces = jnp.transpose(own_state.reshape(mamba_heads, seq_size, rows, NS), (1, 0, 2, 3))
    decays = jnp.broadcast_to(block_decay[None, :, None, None], (seq_size, mamba_heads, 1, NS))
    columns = lax.all_to_all(jnp.concatenate([pieces, decays], axis=2), "seq", 0, 0, tiled=True)
    carry = lax.dynamic_slice_in_dim(ssm_init[0], seq_pos * rows, rows, 1)
    entering = []
    for source in range(seq_size):
        entering.append(carry)
        part = columns[source]
        carry = part[:, rows:, :] * carry + part[:, :rows, :]
    entering = lax.all_to_all(jnp.stack(entering, axis=0), "seq", 0, 0, tiled=True)
    incoming = jnp.transpose(entering, (1, 0, 2, 3)).reshape(mamba_heads, HD, NS)
    carried = jnp.exp(cumulative)[:, :, None] * jnp.einsum(
        "tn,hpn->thp", c_mat, incoming, precision=high
    )
    mamba_y = inner_out + carried + d_skip[None, :, None] * x_conv
    state_after = block_decay[:, None, None] * incoming + own_state
    gated = mamba_y * jax.nn.silu(inner[:, 0].astype(jnp.float32).reshape(tokens, mamba_heads, HD))
    mixed = (
        rms_scale(gated).reshape(tokens, mamba_heads * HD) * mamba_gain.astype(jnp.float32)
    ).astype(jnp.bfloat16)
    cache_rows = cache.shape[1]
    shard_rows = cache_rows + tokens
    group = mp_pos * local_heads // (QH // KVH)
    query_index = seq_pos * tokens + jnp.arange(tokens, dtype=jnp.int32)
    scale = 1.0 / float(HD) ** 0.5
    piece = lax.all_gather(group_rows, "seq", axis=0, tiled=True)
    count = piece.shape[0]
    index = jnp.arange(count, dtype=jnp.int32)
    owner = index // shard_rows
    offset = index % shard_rows
    in_cache = offset < cache_rows
    slot_ok = in_cache & (owner * cache_rows + offset < length)
    new_index = owner * tokens + offset - cache_rows
    never = jnp.iinfo(jnp.int32).max
    key_rank = jnp.where(in_cache, jnp.where(slot_ok, -1, never), new_index)[None, :]
    query_rank = jnp.tile(query_index, local_heads)[:, None]
    query_rows = jnp.transpose(query, (1, 0, 2)).reshape(local_heads * tokens, HD)
    attended = attend(query_rows, query_rank, piece, key_rank, 4 * shard_rows)
    attended = jnp.transpose(attended.reshape(local_heads, tokens, HD), (1, 0, 2)).reshape(
        tokens, local_heads * HD
    )
    attended = attended.astype(jnp.bfloat16)
    term = jnp.dot(attended, w_attn_out, preferred_element_type=jnp.float32)
    term = term + jnp.dot(mixed, w_mamba_out, preferred_element_type=jnp.float32)
    summed = lax.psum_scatter(term, "mp", scatter_dimension=1, tiled=True)
    layer = (summed + own_rows.astype(jnp.float32)).astype(jnp.bfloat16)
    return (layer[None], kv_block[None], state_after[None, None])


def solution(mesh):
    placed = (
        P("req", "seq", "mp"),
        P(),
        P(None, "mp"),
        P(None, "mp"),
        P("mp", None),
        P(None, None, "mp"),
        P(None, "mp"),
        P(None, "mp"),
        P("mp"),
        P("mp"),
        P("mp"),
        P(None, "mp"),
        P(),
        P("mp"),
        P("mp", None),
        P("req", "seq", "mp"),
        P("req"),
        P("req", None, "mp"),
        P("req", None, None),
        P("req", "mp", None, None),
    )
    return jax.shard_map(
        shards,
        mesh=mesh,
        in_specs=placed,
        out_specs=(P("req", "seq", "mp"), P("req", "seq", "mp"), P("req", "seq", "mp", None, None)),
        check_vma=False,
    )
```

```python
import jax
import jax.numpy as jnp
from jax import lax
from jax.sharding import PartitionSpec as P
from jax.experimental import pallas as pl
from jax.experimental.pallas import tpu as pltpu

HD = 128
SEQ = ("seq_hi", "seq_lo")
QH = 8
KVH = 2
NS = 256
CONV = 4


epsilon = 1e-05
rope_base = 100000000000.0
negative = -1e30


def shifted(block, axis, distance):
    devices = range(lax.axis_size(axis))
    route = [(i - distance, i) for i in devices if i - distance in devices]
    return lax.ppermute(block, axis, route)


def prefix(part, axis, combine, identity):
    place = lax.axis_index(axis)
    gathered = jax.tree.map(lambda a: lax.all_gather(a, axis), part)
    state = jax.tree.map(lambda a, e: jnp.zeros_like(a) + jnp.asarray(e, a.dtype), part, identity)

    def one(turn, state):
        return combine(
            state, jax.tree.map(lambda a: lax.dynamic_index_in_dim(a, turn, 0, False), gathered)
        )

    return lax.fori_loop(0, place, one, state)


def attend(query_rows, query_rank, pieces, key_rank, block):
    rows = query_rows.shape[0]
    count = pieces.shape[0]
    steps = count // block
    scale = 1.0 / float(HD) ** 0.5

    def kernel(qr_ref, q_ref, kr_ref, kv_ref, out_ref, top_ref, total_ref, acc_ref):
        step = pl.program_id(0)

        @pl.when(step == 0)
        def _():
            top_ref[...] = jnp.full(top_ref.shape, negative, jnp.float32)
            total_ref[...] = jnp.zeros(total_ref.shape, jnp.float32)
            acc_ref[...] = jnp.zeros(acc_ref.shape, jnp.float32)

        scores = lax.dot_general(
            q_ref[...], kv_ref[:, :HD], (((1,), (1,)), ((), ())), preferred_element_type=jnp.float32
        ) * scale
        valid = kr_ref[...] <= qr_ref[...]
        masked = jnp.where(valid, scores, negative)
        old = top_ref[...]
        new = jnp.maximum(old, jnp.max(masked, axis=1, keepdims=True))
        weights = jnp.where(valid, jnp.exp(masked - new), 0.0)
        alpha = jnp.exp(old - new)
        total_ref[...] = alpha * total_ref[...] + jnp.sum(weights, axis=1, keepdims=True)
        acc_ref[...] = alpha * acc_ref[...] + jnp.dot(
            weights.astype(jnp.bfloat16), kv_ref[:, HD:], preferred_element_type=jnp.float32
        )
        top_ref[...] = new

        @pl.when(step == steps - 1)
        def _():
            out_ref[...] = (acc_ref[...] / total_ref[...]).astype(out_ref.dtype)

    return pl.pallas_call(
        kernel,
        grid=(steps,),
        in_specs=[
            pl.BlockSpec((rows, 1), lambda i: (0, 0)),
            pl.BlockSpec((rows, HD), lambda i: (0, 0)),
            pl.BlockSpec((1, block), lambda i: (0, i)),
            pl.BlockSpec((block, 2 * HD), lambda i: (i, 0)),
        ],
        out_specs=pl.BlockSpec((rows, HD), lambda i: (0, 0)),
        out_shape=jax.ShapeDtypeStruct((rows, HD), jnp.bfloat16),
        scratch_shapes=[
            pltpu.VMEM((rows, 1), jnp.float32),
            pltpu.VMEM((rows, 1), jnp.float32),
            pltpu.VMEM((rows, HD), jnp.float32),
        ],
        compiler_params=pltpu.CompilerParams(vmem_limit_bytes=48 * 1024 * 1024),
    )(query_rank, query_rows, key_rank, pieces)


def rotate(values, positions):
    half = HD // 2
    freqs = rope_base ** (-jnp.arange(half, dtype=jnp.float32) * 2.0 / HD)
    angles = positions.astype(jnp.float32)[:, None] * freqs[None, :]
    cosine = jnp.cos(angles)[:, None, :]
    sine = jnp.sin(angles)[:, None, :]
    first = values[..., :half]
    second = values[..., half:]
    return jnp.concatenate(
        [first * cosine - second * sine, second * cosine + first * sine], axis=-1
    )


def rms_scale(values):
    mean_sq = jnp.mean(values * values, axis=-1, keepdims=True)
    return values * lax.rsqrt(mean_sq + epsilon)


def causal_conv(tail, inputs, taps):
    padded = jnp.concatenate([tail, inputs], axis=0).astype(jnp.float32)
    count = inputs.shape[0]
    total = jnp.zeros(inputs.shape, jnp.float32)
    for offset in range(CONV):
        total = total + taps[offset].astype(jnp.float32)[None, :] * padded[offset : offset + count]
    return jax.nn.silu(total)


def join_states(earlier, later):
    return (earlier[0] * later[0], later[0][:, None, None] * earlier[1] + later[1])


def shards(
    hidden,
    norm_gain,
    w_query,
    w_keyval,
    w_attn_out,
    w_inner,
    w_bc,
    w_dt,
    dt_bias,
    a_log,
    d_skip,
    conv_x,
    conv_bc,
    mamba_gain,
    w_mamba_out,
    cache,
    cache_len,
    tail_x,
    tail_bc,
    ssm_init,
):
    high = lax.Precision.HIGHEST
    own_rows = hidden[0]
    tokens = own_rows.shape[0]
    seq_pos = lax.axis_index(SEQ)
    mp_pos = lax.axis_index("mp")
    length = cache_len[0]
    whole = lax.all_gather(own_rows, "mp", axis=1, tiled=True)
    normed = (rms_scale(whole.astype(jnp.float32)) * norm_gain.astype(jnp.float32)).astype(
        jnp.bfloat16
    )
    positions = length + seq_pos * tokens + jnp.arange(tokens, dtype=jnp.int32)
    local_heads = w_query.shape[1] // HD
    query = rotate(
        jnp.dot(normed, w_query, preferred_element_type=jnp.float32).reshape(
            tokens, local_heads, HD
        ),
        positions,
    ).astype(jnp.bfloat16)
    projected = jnp.dot(normed, w_keyval, preferred_element_type=jnp.float32)
    roped = rotate(projected[:, None, :], positions)[:, 0, :]
    kv_block = jnp.where(mp_pos % 2 == 0, roped, projected).astype(jnp.bfloat16)
    bc_block = jnp.dot(normed, w_bc, preferred_element_type=jnp.float32).astype(jnp.bfloat16)
    bc_all = lax.all_gather(bc_block, "mp", axis=1, tiled=True)
    own_rows_kv = jnp.concatenate([cache[0], kv_block], axis=0)
    mp_size = lax.axis_size("mp")
    partner = lax.ppermute(own_rows_kv, "mp", [(i, i ^ 1) for i in range(mp_size)])
    is_key_block = mp_pos % 2 == 0
    group_rows = jnp.where(
        is_key_block,
        jnp.concatenate([own_rows_kv, partner], axis=1),
        jnp.concatenate([partner, own_rows_kv], axis=1),
    )
    inner = jnp.einsum("td,dkc->tkc", normed, w_inner, preferred_element_type=jnp.float32).astype(
        jnp.bfloat16
    )
    rim = CONV - 1
    prev_x, prev_bc = shifted((inner[tokens - rim :, 1], bc_all[tokens - rim :]), SEQ, 1)
    first_block = seq_pos == 0
    prev_x = jnp.where(first_block, tail_x[0], prev_x)
    prev_bc = jnp.where(first_block, tail_bc[0], prev_bc)
    mamba_heads = dt_bias.shape[0]
    x_conv = causal_conv(prev_x, inner[:, 1], conv_x).reshape(tokens, mamba_heads, HD)
    bc_conv = causal_conv(prev_bc, bc_all, conv_bc)
    b_mat = bc_conv[:, :NS]
    c_mat = bc_conv[:, NS:]
    step_size = jax.nn.softplus(jnp.dot(normed, w_dt, preferred_element_type=jnp.float32) + dt_bias)
    log_decay = -step_size * jnp.exp(a_log)[None, :]
    cumulative = jnp.cumsum(log_decay, axis=0)
    pairs = jnp.dot(c_mat, b_mat.T, precision=high)
    gap = cumulative[:, None, :] - cumulative[None, :, :]
    token_ids = jnp.arange(tokens)
    lower = (token_ids[:, None] >= token_ids[None, :])[:, :, None]
    decay = jnp.where(lower, jnp.exp(jnp.where(lower, gap, 0.0)), 0.0)
    mixing = decay * pairs[:, :, None] * step_size[None, :, :]
    inner_out = jnp.einsum("tsh,shp->thp", mixing, x_conv, precision=high)
    to_end = jnp.exp(cumulative[-1][None, :] - cumulative) * step_size
    own_state = jnp.einsum("sh,shp,sn->hpn", to_end, x_conv, b_mat, precision=high)
    block_decay = jnp.exp(cumulative[-1])
    seq_size = lax.axis_size(SEQ)
    rows = HD // seq_size
    pieces = jnp.transpose(own_state.reshape(mamba_heads, seq_size, rows, NS), (1, 0, 2, 3))
    decays = jnp.broadcast_to(block_decay[None, :, None, None], (seq_size, mamba_heads, 1, NS))
    columns = lax.all_to_all(jnp.concatenate([pieces, decays], axis=2), SEQ, 0, 0, tiled=True)
    carry = lax.dynamic_slice_in_dim(ssm_init[0], seq_pos * rows, rows, 1)
    entering = []
    for source in range(seq_size):
        entering.append(carry)
        part = columns[source]
        carry = part[:, rows:, :] * carry + part[:, :rows, :]
    entering = lax.all_to_all(jnp.stack(entering, axis=0), SEQ, 0, 0, tiled=True)
    incoming = jnp.transpose(entering, (1, 0, 2, 3)).reshape(mamba_heads, HD, NS)
    carried = jnp.exp(cumulative)[:, :, None] * jnp.einsum(
        "tn,hpn->thp", c_mat, incoming, precision=high
    )
    mamba_y = inner_out + carried + d_skip[None, :, None] * x_conv
    state_after = block_decay[:, None, None] * incoming + own_state
    gated = mamba_y * jax.nn.silu(inner[:, 0].astype(jnp.float32).reshape(tokens, mamba_heads, HD))
    mixed = (
        rms_scale(gated).reshape(tokens, mamba_heads * HD) * mamba_gain.astype(jnp.float32)
    ).astype(jnp.bfloat16)
    cache_rows = cache.shape[1]
    shard_rows = cache_rows + tokens
    group = mp_pos * local_heads // (QH // KVH)
    query_index = seq_pos * tokens + jnp.arange(tokens, dtype=jnp.int32)
    scale = 1.0 / float(HD) ** 0.5
    piece = lax.all_gather(group_rows, SEQ[1], axis=0, tiled=True)
    piece = lax.all_gather(piece, SEQ[0], axis=0, tiled=True)
    count = piece.shape[0]
    index = jnp.arange(count, dtype=jnp.int32)
    owner = index // shard_rows
    offset = index % shard_rows
    in_cache = offset < cache_rows
    slot_ok = in_cache & (owner * cache_rows + offset < length)
    new_index = owner * tokens + offset - cache_rows
    never = jnp.iinfo(jnp.int32).max
    key_rank = jnp.where(in_cache, jnp.where(slot_ok, -1, never), new_index)[None, :]
    query_rank = jnp.tile(query_index, local_heads)[:, None]
    query_rows = jnp.transpose(query, (1, 0, 2)).reshape(local_heads * tokens, HD)
    attended = attend(query_rows, query_rank, piece, key_rank, 4 * shard_rows)
    attended = jnp.transpose(attended.reshape(local_heads, tokens, HD), (1, 0, 2)).reshape(
        tokens, local_heads * HD
    )
    attended = attended.astype(jnp.bfloat16)
    term = jnp.dot(attended, w_attn_out, preferred_element_type=jnp.float32)
    term = term + jnp.dot(mixed, w_mamba_out, preferred_element_type=jnp.float32)
    summed = lax.psum_scatter(term, "mp", scatter_dimension=1, tiled=True)
    layer = (summed + own_rows.astype(jnp.float32)).astype(jnp.bfloat16)
    return (layer[None], kv_block[None], state_after[None, None])


def solution(mesh):
    devices = mesh.devices
    lanes = devices[:, 0, 0]
    inner = len({d.coords[1] for d in lanes}) if hasattr(lanes[0], "coords") else 1
    split = jax.sharding.Mesh(
        devices.reshape((devices.shape[0] // inner, inner) + devices.shape[1:]), SEQ + mesh.axis_names[1:]
    )
    placed = (
        P("req", SEQ, "mp"),
        P(),
        P(None, "mp"),
        P(None, "mp"),
        P("mp", None),
        P(None, None, "mp"),
        P(None, "mp"),
        P(None, "mp"),
        P("mp"),
        P("mp"),
        P("mp"),
        P(None, "mp"),
        P(),
        P("mp"),
        P("mp", None),
        P("req", SEQ, "mp"),
        P("req"),
        P("req", None, "mp"),
        P("req", None, None),
        P("req", "mp", None, None),
    )
    return jax.shard_map(
        shards,
        mesh=split,
        in_specs=placed,
        out_specs=(P("req", SEQ, "mp"), P("req", SEQ, "mp"), P("req", SEQ, "mp", None, None)),
        check_vma=False,
    )
```

```python
import jax
import jax.numpy as jnp
from jax import lax
from jax.sharding import PartitionSpec as P
from jax.experimental import pallas as pl
from jax.experimental.pallas import tpu as pltpu

HD = 128
QH = 8
KVH = 2
NS = 256
CONV = 4


epsilon = 1e-05
rope_base = 100000000000.0
negative = -1e30


def shifted(block, axis, distance):
    devices = range(lax.axis_size(axis))
    route = [(i - distance, i) for i in devices if i - distance in devices]
    return lax.ppermute(block, axis, route)


def prefix(part, axis, combine, identity):
    place = lax.axis_index(axis)
    gathered = jax.tree.map(lambda a: lax.all_gather(a, axis), part)
    state = jax.tree.map(lambda a, e: jnp.zeros_like(a) + jnp.asarray(e, a.dtype), part, identity)

    def one(turn, state):
        return combine(
            state, jax.tree.map(lambda a: lax.dynamic_index_in_dim(a, turn, 0, False), gathered)
        )

    return lax.fori_loop(0, place, one, state)


def attend(query_rows, query_rank, pieces, key_rank, block):
    rows = query_rows.shape[0]
    count = pieces.shape[0]
    steps = count // block
    scale = 1.0 / float(HD) ** 0.5

    def kernel(qr_ref, q_ref, kr_ref, kv_ref, out_ref, top_ref, total_ref, acc_ref):
        step = pl.program_id(0)

        @pl.when(step == 0)
        def _():
            top_ref[...] = jnp.full(top_ref.shape, negative, jnp.float32)
            total_ref[...] = jnp.zeros(total_ref.shape, jnp.float32)
            acc_ref[...] = jnp.zeros(acc_ref.shape, jnp.float32)

        scores = lax.dot_general(
            q_ref[...], kv_ref[:, :HD], (((1,), (1,)), ((), ())), preferred_element_type=jnp.float32
        ) * scale
        valid = kr_ref[...] <= qr_ref[...]
        masked = jnp.where(valid, scores, negative)
        old = top_ref[...]
        new = jnp.maximum(old, jnp.max(masked, axis=1, keepdims=True))
        weights = jnp.where(valid, jnp.exp(masked - new), 0.0)
        alpha = jnp.exp(old - new)
        total_ref[...] = alpha * total_ref[...] + jnp.sum(weights, axis=1, keepdims=True)
        acc_ref[...] = alpha * acc_ref[...] + jnp.dot(
            weights.astype(jnp.bfloat16), kv_ref[:, HD:], preferred_element_type=jnp.float32
        )
        top_ref[...] = new

        @pl.when(step == steps - 1)
        def _():
            out_ref[...] = (acc_ref[...] / total_ref[...]).astype(out_ref.dtype)

    return pl.pallas_call(
        kernel,
        grid=(steps,),
        in_specs=[
            pl.BlockSpec((rows, 1), lambda i: (0, 0)),
            pl.BlockSpec((rows, HD), lambda i: (0, 0)),
            pl.BlockSpec((1, block), lambda i: (0, i)),
            pl.BlockSpec((block, 2 * HD), lambda i: (i, 0)),
        ],
        out_specs=pl.BlockSpec((rows, HD), lambda i: (0, 0)),
        out_shape=jax.ShapeDtypeStruct((rows, HD), jnp.bfloat16),
        scratch_shapes=[
            pltpu.VMEM((rows, 1), jnp.float32),
            pltpu.VMEM((rows, 1), jnp.float32),
            pltpu.VMEM((rows, HD), jnp.float32),
        ],
        compiler_params=pltpu.CompilerParams(vmem_limit_bytes=48 * 1024 * 1024),
    )(query_rank, query_rows, key_rank, pieces)


def rotate(values, positions):
    half = HD // 2
    freqs = rope_base ** (-jnp.arange(half, dtype=jnp.float32) * 2.0 / HD)
    angles = positions.astype(jnp.float32)[:, None] * freqs[None, :]
    cosine = jnp.cos(angles)[:, None, :]
    sine = jnp.sin(angles)[:, None, :]
    first = values[..., :half]
    second = values[..., half:]
    return jnp.concatenate(
        [first * cosine - second * sine, second * cosine + first * sine], axis=-1
    )


def rms_scale(values):
    mean_sq = jnp.mean(values * values, axis=-1, keepdims=True)
    return values * lax.rsqrt(mean_sq + epsilon)


def causal_conv(tail, inputs, taps):
    padded = jnp.concatenate([tail, inputs], axis=0).astype(jnp.float32)
    count = inputs.shape[0]
    total = jnp.zeros(inputs.shape, jnp.float32)
    for offset in range(CONV):
        total = total + taps[offset].astype(jnp.float32)[None, :] * padded[offset : offset + count]
    return jax.nn.silu(total)


def join_states(earlier, later):
    return (earlier[0] * later[0], later[0][:, None, None] * earlier[1] + later[1])


def shards(
    hidden,
    norm_gain,
    w_query,
    w_keyval,
    w_attn_out,
    w_inner,
    w_bc,
    w_dt,
    dt_bias,
    a_log,
    d_skip,
    conv_x,
    conv_bc,
    mamba_gain,
    w_mamba_out,
    cache,
    cache_len,
    tail_x,
    tail_bc,
    ssm_init,
):
    high = lax.Precision.HIGHEST
    own_rows = hidden[0]
    tokens = own_rows.shape[0]
    seq_pos = lax.axis_index("seq")
    mp_pos = lax.axis_index("mp")
    length = cache_len[0]
    whole = lax.all_gather(own_rows, "mp", axis=1, tiled=True)
    normed = (rms_scale(whole.astype(jnp.float32)) * norm_gain.astype(jnp.float32)).astype(
        jnp.bfloat16
    )
    positions = length + seq_pos * tokens + jnp.arange(tokens, dtype=jnp.int32)
    local_heads = w_query.shape[1] // HD
    query = rotate(
        jnp.dot(normed, w_query, preferred_element_type=jnp.float32).reshape(
            tokens, local_heads, HD
        ),
        positions,
    ).astype(jnp.bfloat16)
    projected = jnp.dot(normed, w_keyval, preferred_element_type=jnp.float32)
    roped = rotate(projected[:, None, :], positions)[:, 0, :]
    kv_block = jnp.where(mp_pos % 2 == 0, roped, projected).astype(jnp.bfloat16)
    bc_block = jnp.dot(normed, w_bc, preferred_element_type=jnp.float32).astype(jnp.bfloat16)
    bc_all = lax.all_gather(bc_block, "mp", axis=1, tiled=True)
    own_rows_kv = jnp.concatenate([cache[0], kv_block], axis=0)
    mp_size = lax.axis_size("mp")
    partner = lax.ppermute(own_rows_kv, "mp", [(i, i ^ 1) for i in range(mp_size)])
    is_key_block = mp_pos % 2 == 0
    group_rows = jnp.where(
        is_key_block,
        jnp.concatenate([own_rows_kv, partner], axis=1),
        jnp.concatenate([partner, own_rows_kv], axis=1),
    )
    inner = jnp.einsum("td,dkc->tkc", normed, w_inner, preferred_element_type=jnp.float32).astype(
        jnp.bfloat16
    )
    rim = CONV - 1
    prev_x, prev_bc = shifted((inner[tokens - rim :, 1], bc_all[tokens - rim :]), "seq", 1)
    first_block = seq_pos == 0
    prev_x = jnp.where(first_block, tail_x[0], prev_x)
    prev_bc = jnp.where(first_block, tail_bc[0], prev_bc)
    mamba_heads = dt_bias.shape[0]
    x_conv = causal_conv(prev_x, inner[:, 1], conv_x).reshape(tokens, mamba_heads, HD)
    bc_conv = causal_conv(prev_bc, bc_all, conv_bc)
    b_mat = bc_conv[:, :NS]
    c_mat = bc_conv[:, NS:]
    step_size = jax.nn.softplus(jnp.dot(normed, w_dt, preferred_element_type=jnp.float32) + dt_bias)
    log_decay = -step_size * jnp.exp(a_log)[None, :]
    cumulative = jnp.cumsum(log_decay, axis=0)
    pairs = jnp.dot(c_mat, b_mat.T, precision=high)
    gap = cumulative[:, None, :] - cumulative[None, :, :]
    token_ids = jnp.arange(tokens)
    lower = (token_ids[:, None] >= token_ids[None, :])[:, :, None]
    decay = jnp.where(lower, jnp.exp(jnp.where(lower, gap, 0.0)), 0.0)
    mixing = decay * pairs[:, :, None] * step_size[None, :, :]
    inner_out = jnp.einsum("tsh,shp->thp", mixing, x_conv, precision=high)
    to_end = jnp.exp(cumulative[-1][None, :] - cumulative) * step_size
    own_state = jnp.einsum("sh,shp,sn->hpn", to_end, x_conv, b_mat, precision=high)
    block_decay = jnp.exp(cumulative[-1])
    seq_size = lax.axis_size("seq")
    rows = HD // seq_size
    pieces = jnp.transpose(own_state.reshape(mamba_heads, seq_size, rows, NS), (1, 0, 2, 3))
    decays = jnp.broadcast_to(block_decay[None, :, None, None], (seq_size, mamba_heads, 1, NS))
    columns = lax.all_to_all(jnp.concatenate([pieces, decays], axis=2), "seq", 0, 0, tiled=True)
    carry = lax.dynamic_slice_in_dim(ssm_init[0], seq_pos * rows, rows, 1)
    entering = []
    for source in range(seq_size):
        entering.append(carry)
        part = columns[source]
        carry = part[:, rows:, :] * carry + part[:, :rows, :]
    entering = lax.all_to_all(jnp.stack(entering, axis=0), "seq", 0, 0, tiled=True)
    incoming = jnp.transpose(entering, (1, 0, 2, 3)).reshape(mamba_heads, HD, NS)
    carried = jnp.exp(cumulative)[:, :, None] * jnp.einsum(
        "tn,hpn->thp", c_mat, incoming, precision=high
    )
    mamba_y = inner_out + carried + d_skip[None, :, None] * x_conv
    state_after = block_decay[:, None, None] * incoming + own_state
    gated = mamba_y * jax.nn.silu(inner[:, 0].astype(jnp.float32).reshape(tokens, mamba_heads, HD))
    mixed = (
        rms_scale(gated).reshape(tokens, mamba_heads * HD) * mamba_gain.astype(jnp.float32)
    ).astype(jnp.bfloat16)
    cache_rows = cache.shape[1]
    shard_rows = cache_rows + tokens
    group = mp_pos * local_heads // (QH // KVH)
    query_index = seq_pos * tokens + jnp.arange(tokens, dtype=jnp.int32)
    scale = 1.0 / float(HD) ** 0.5
    piece = lax.all_gather(group_rows, "seq", axis=0, tiled=True)
    count = piece.shape[0]
    index = jnp.arange(count, dtype=jnp.int32)
    owner = index // shard_rows
    offset = index % shard_rows
    in_cache = offset < cache_rows
    slot_ok = in_cache & (owner * cache_rows + offset < length)
    new_index = owner * tokens + offset - cache_rows
    never = jnp.iinfo(jnp.int32).max
    key_rank = jnp.where(in_cache, jnp.where(slot_ok, -1, never), new_index)[None, :]
    query_rank = jnp.tile(query_index, local_heads)[:, None]
    query_rows = jnp.transpose(query, (1, 0, 2)).reshape(local_heads * tokens, HD)
    attended = attend(query_rows, query_rank, piece, key_rank, 4 * shard_rows)
    attended = jnp.transpose(attended.reshape(local_heads, tokens, HD), (1, 0, 2)).reshape(
        tokens, local_heads * HD
    )
    attended = attended.astype(jnp.bfloat16)
    term = jnp.dot(attended, w_attn_out, preferred_element_type=jnp.float32)
    term = term + jnp.dot(mixed, w_mamba_out, preferred_element_type=jnp.float32)
    summed = lax.psum_scatter(term.astype(jnp.bfloat16), "mp", scatter_dimension=1, tiled=True)
    summed = summed.astype(jnp.float32)
    layer = (summed + own_rows.astype(jnp.float32)).astype(jnp.bfloat16)
    return (layer[None], kv_block[None], state_after[None, None])


def solution(mesh):
    placed = (
        P("req", "seq", "mp"),
        P(),
        P(None, "mp"),
        P(None, "mp"),
        P("mp", None),
        P(None, None, "mp"),
        P(None, "mp"),
        P(None, "mp"),
        P("mp"),
        P("mp"),
        P("mp"),
        P(None, "mp"),
        P(),
        P("mp"),
        P("mp", None),
        P("req", "seq", "mp"),
        P("req"),
        P("req", None, "mp"),
        P("req", None, None),
        P("req", "mp", None, None),
    )
    return jax.shard_map(
        shards,
        mesh=mesh,
        in_specs=placed,
        out_specs=(P("req", "seq", "mp"), P("req", "seq", "mp"), P("req", "seq", "mp", None, None)),
        check_vma=False,
    )
```

```python
import jax
import jax.numpy as jnp
from jax import lax
from jax.sharding import PartitionSpec as P
from jax.experimental import pallas as pl
from jax.experimental.pallas import tpu as pltpu

HD = 128
QH = 8
KVH = 2
NS = 256
CONV = 4


epsilon = 1e-05
rope_base = 100000000000.0
negative = -1e30


def shifted(block, axis, distance):
    devices = range(lax.axis_size(axis))
    route = [(i - distance, i) for i in devices if i - distance in devices]
    return lax.ppermute(block, axis, route)


def prefix(part, axis, combine, identity):
    place = lax.axis_index(axis)
    gathered = jax.tree.map(lambda a: lax.all_gather(a, axis), part)
    state = jax.tree.map(lambda a, e: jnp.zeros_like(a) + jnp.asarray(e, a.dtype), part, identity)

    def one(turn, state):
        return combine(
            state, jax.tree.map(lambda a: lax.dynamic_index_in_dim(a, turn, 0, False), gathered)
        )

    return lax.fori_loop(0, place, one, state)


def attend(query_rows, query_rank, pieces, key_rank, block):
    rows = query_rows.shape[0]
    count = pieces.shape[0]
    steps = count // block
    scale = 1.0 / float(HD) ** 0.5

    def kernel(qr_ref, q_ref, kr_ref, kv_ref, out_ref, top_ref, total_ref, acc_ref):
        step = pl.program_id(0)

        @pl.when(step == 0)
        def _():
            top_ref[...] = jnp.full(top_ref.shape, negative, jnp.float32)
            total_ref[...] = jnp.zeros(total_ref.shape, jnp.float32)
            acc_ref[...] = jnp.zeros(acc_ref.shape, jnp.float32)

        scores = lax.dot_general(
            q_ref[...], kv_ref[:, :HD], (((1,), (1,)), ((), ())), preferred_element_type=jnp.float32
        ) * scale
        valid = kr_ref[...] <= qr_ref[...]
        masked = jnp.where(valid, scores, negative)
        old = top_ref[...]
        new = jnp.maximum(old, jnp.max(masked, axis=1, keepdims=True))
        weights = jnp.where(valid, jnp.exp(masked - new), 0.0)
        alpha = jnp.exp(old - new)
        total_ref[...] = alpha * total_ref[...] + jnp.sum(weights, axis=1, keepdims=True)
        acc_ref[...] = alpha * acc_ref[...] + jnp.dot(
            weights.astype(jnp.bfloat16), kv_ref[:, HD:], preferred_element_type=jnp.float32
        )
        top_ref[...] = new

        @pl.when(step == steps - 1)
        def _():
            out_ref[...] = (acc_ref[...] / total_ref[...]).astype(out_ref.dtype)

    return pl.pallas_call(
        kernel,
        grid=(steps,),
        in_specs=[
            pl.BlockSpec((rows, 1), lambda i: (0, 0)),
            pl.BlockSpec((rows, HD), lambda i: (0, 0)),
            pl.BlockSpec((1, block), lambda i: (0, i)),
            pl.BlockSpec((block, 2 * HD), lambda i: (i, 0)),
        ],
        out_specs=pl.BlockSpec((rows, HD), lambda i: (0, 0)),
        out_shape=jax.ShapeDtypeStruct((rows, HD), jnp.bfloat16),
        scratch_shapes=[
            pltpu.VMEM((rows, 1), jnp.float32),
            pltpu.VMEM((rows, 1), jnp.float32),
            pltpu.VMEM((rows, HD), jnp.float32),
        ],
        compiler_params=pltpu.CompilerParams(vmem_limit_bytes=48 * 1024 * 1024),
    )(query_rank, query_rows, key_rank, pieces)


def rotate(values, positions):
    half = HD // 2
    freqs = rope_base ** (-jnp.arange(half, dtype=jnp.float32) * 2.0 / HD)
    angles = positions.astype(jnp.float32)[:, None] * freqs[None, :]
    cosine = jnp.cos(angles)[:, None, :]
    sine = jnp.sin(angles)[:, None, :]
    first = values[..., :half]
    second = values[..., half:]
    return jnp.concatenate(
        [first * cosine - second * sine, second * cosine + first * sine], axis=-1
    )


def rms_scale(values):
    mean_sq = jnp.mean(values * values, axis=-1, keepdims=True)
    return values * lax.rsqrt(mean_sq + epsilon)


def causal_conv(tail, inputs, taps):
    padded = jnp.concatenate([tail, inputs], axis=0).astype(jnp.float32)
    count = inputs.shape[0]
    total = jnp.zeros(inputs.shape, jnp.float32)
    for offset in range(CONV):
        total = total + taps[offset].astype(jnp.float32)[None, :] * padded[offset : offset + count]
    return jax.nn.silu(total)


def join_states(earlier, later):
    return (earlier[0] * later[0], later[0][:, None, None] * earlier[1] + later[1])


def shards(
    hidden,
    norm_gain,
    w_query,
    w_keyval,
    w_attn_out,
    w_inner,
    w_bc,
    w_dt,
    dt_bias,
    a_log,
    d_skip,
    conv_x,
    conv_bc,
    mamba_gain,
    w_mamba_out,
    cache,
    cache_len,
    tail_x,
    tail_bc,
    ssm_init,
):
    high = lax.Precision.HIGHEST
    own_rows = hidden[0]
    tokens = own_rows.shape[0]
    seq_pos = lax.axis_index("seq")
    mp_pos = lax.axis_index("mp")
    length = cache_len[0]
    mp_count = lax.axis_size("mp")
    width = own_rows.shape[1]
    whole = jnp.zeros((tokens, mp_count * width), own_rows.dtype)
    for shift in range(mp_count):
        if shift == 0:
            part = own_rows
        else:
            part = lax.ppermute(own_rows, "mp", [(i, (i + shift) % mp_count) for i in range(mp_count)])
        source = (lax.axis_index("mp") + mp_count - shift) % mp_count
        whole = lax.dynamic_update_slice(whole, part, (0, source * width))
    normed = (rms_scale(whole.astype(jnp.float32)) * norm_gain.astype(jnp.float32)).astype(
        jnp.bfloat16
    )
    positions = length + seq_pos * tokens + jnp.arange(tokens, dtype=jnp.int32)
    local_heads = w_query.shape[1] // HD
    query = rotate(
        jnp.dot(normed, w_query, preferred_element_type=jnp.float32).reshape(
            tokens, local_heads, HD
        ),
        positions,
    ).astype(jnp.bfloat16)
    projected = jnp.dot(normed, w_keyval, preferred_element_type=jnp.float32)
    roped = rotate(projected[:, None, :], positions)[:, 0, :]
    kv_block = jnp.where(mp_pos % 2 == 0, roped, projected).astype(jnp.bfloat16)
    bc_block = jnp.dot(normed, w_bc, preferred_element_type=jnp.float32).astype(jnp.bfloat16)
    bc_all = lax.all_gather(bc_block, "mp", axis=1, tiled=True)
    own_rows_kv = jnp.concatenate([cache[0], kv_block], axis=0)
    mp_size = lax.axis_size("mp")
    partner = lax.ppermute(own_rows_kv, "mp", [(i, i ^ 1) for i in range(mp_size)])
    is_key_block = mp_pos % 2 == 0
    group_rows = jnp.where(
        is_key_block,
        jnp.concatenate([own_rows_kv, partner], axis=1),
        jnp.concatenate([partner, own_rows_kv], axis=1),
    )
    inner = jnp.einsum("td,dkc->tkc", normed, w_inner, preferred_element_type=jnp.float32).astype(
        jnp.bfloat16
    )
    rim = CONV - 1
    prev_x, prev_bc = shifted((inner[tokens - rim :, 1], bc_all[tokens - rim :]), "seq", 1)
    first_block = seq_pos == 0
    prev_x = jnp.where(first_block, tail_x[0], prev_x)
    prev_bc = jnp.where(first_block, tail_bc[0], prev_bc)
    mamba_heads = dt_bias.shape[0]
    x_conv = causal_conv(prev_x, inner[:, 1], conv_x).reshape(tokens, mamba_heads, HD)
    bc_conv = causal_conv(prev_bc, bc_all, conv_bc)
    b_mat = bc_conv[:, :NS]
    c_mat = bc_conv[:, NS:]
    step_size = jax.nn.softplus(jnp.dot(normed, w_dt, preferred_element_type=jnp.float32) + dt_bias)
    log_decay = -step_size * jnp.exp(a_log)[None, :]
    cumulative = jnp.cumsum(log_decay, axis=0)
    pairs = jnp.dot(c_mat, b_mat.T, precision=high)
    gap = cumulative[:, None, :] - cumulative[None, :, :]
    token_ids = jnp.arange(tokens)
    lower = (token_ids[:, None] >= token_ids[None, :])[:, :, None]
    decay = jnp.where(lower, jnp.exp(jnp.where(lower, gap, 0.0)), 0.0)
    mixing = decay * pairs[:, :, None] * step_size[None, :, :]
    inner_out = jnp.einsum("tsh,shp->thp", mixing, x_conv, precision=high)
    to_end = jnp.exp(cumulative[-1][None, :] - cumulative) * step_size
    own_state = jnp.einsum("sh,shp,sn->hpn", to_end, x_conv, b_mat, precision=high)
    block_decay = jnp.exp(cumulative[-1])
    seq_size = lax.axis_size("seq")
    rows = HD // seq_size
    pieces = jnp.transpose(own_state.reshape(mamba_heads, seq_size, rows, NS), (1, 0, 2, 3))
    decays = jnp.broadcast_to(block_decay[None, :, None, None], (seq_size, mamba_heads, 1, NS))
    columns = lax.all_to_all(jnp.concatenate([pieces, decays], axis=2), "seq", 0, 0, tiled=True)
    carry = lax.dynamic_slice_in_dim(ssm_init[0], seq_pos * rows, rows, 1)
    entering = []
    for source in range(seq_size):
        entering.append(carry)
        part = columns[source]
        carry = part[:, rows:, :] * carry + part[:, :rows, :]
    entering = lax.all_to_all(jnp.stack(entering, axis=0), "seq", 0, 0, tiled=True)
    incoming = jnp.transpose(entering, (1, 0, 2, 3)).reshape(mamba_heads, HD, NS)
    carried = jnp.exp(cumulative)[:, :, None] * jnp.einsum(
        "tn,hpn->thp", c_mat, incoming, precision=high
    )
    mamba_y = inner_out + carried + d_skip[None, :, None] * x_conv
    state_after = block_decay[:, None, None] * incoming + own_state
    gated = mamba_y * jax.nn.silu(inner[:, 0].astype(jnp.float32).reshape(tokens, mamba_heads, HD))
    mixed = (
        rms_scale(gated).reshape(tokens, mamba_heads * HD) * mamba_gain.astype(jnp.float32)
    ).astype(jnp.bfloat16)
    cache_rows = cache.shape[1]
    shard_rows = cache_rows + tokens
    group = mp_pos * local_heads // (QH // KVH)
    query_index = seq_pos * tokens + jnp.arange(tokens, dtype=jnp.int32)
    scale = 1.0 / float(HD) ** 0.5
    piece = lax.all_gather(group_rows, "seq", axis=0, tiled=True)
    count = piece.shape[0]
    index = jnp.arange(count, dtype=jnp.int32)
    owner = index // shard_rows
    offset = index % shard_rows
    in_cache = offset < cache_rows
    slot_ok = in_cache & (owner * cache_rows + offset < length)
    new_index = owner * tokens + offset - cache_rows
    never = jnp.iinfo(jnp.int32).max
    key_rank = jnp.where(in_cache, jnp.where(slot_ok, -1, never), new_index)[None, :]
    query_rank = jnp.tile(query_index, local_heads)[:, None]
    query_rows = jnp.transpose(query, (1, 0, 2)).reshape(local_heads * tokens, HD)
    attended = attend(query_rows, query_rank, piece, key_rank, 4 * shard_rows)
    attended = jnp.transpose(attended.reshape(local_heads, tokens, HD), (1, 0, 2)).reshape(
        tokens, local_heads * HD
    )
    attended = attended.astype(jnp.bfloat16)
    term = jnp.dot(attended, w_attn_out, preferred_element_type=jnp.float32)
    term = term + jnp.dot(mixed, w_mamba_out, preferred_element_type=jnp.float32)
    summed = lax.psum_scatter(term.astype(jnp.bfloat16), "mp", scatter_dimension=1, tiled=True)
    summed = summed.astype(jnp.float32)
    layer = (summed + own_rows.astype(jnp.float32)).astype(jnp.bfloat16)
    return (layer[None], kv_block[None], state_after[None, None])


def solution(mesh):
    placed = (
        P("req", "seq", "mp"),
        P(),
        P(None, "mp"),
        P(None, "mp"),
        P("mp", None),
        P(None, None, "mp"),
        P(None, "mp"),
        P(None, "mp"),
        P("mp"),
        P("mp"),
        P("mp"),
        P(None, "mp"),
        P(),
        P("mp"),
        P("mp", None),
        P("req", "seq", "mp"),
        P("req"),
        P("req", None, "mp"),
        P("req", None, None),
        P("req", "mp", None, None),
    )
    return jax.shard_map(
        shards,
        mesh=mesh,
        in_specs=placed,
        out_specs=(P("req", "seq", "mp"), P("req", "seq", "mp"), P("req", "seq", "mp", None, None)),
        check_vma=False,
    )
```

```python
import jax
import jax.numpy as jnp
from jax import lax
from jax.sharding import PartitionSpec as P
from jax.experimental import pallas as pl
from jax.experimental.pallas import tpu as pltpu

HD = 128
QH = 8
KVH = 2
NS = 256
CONV = 4


epsilon = 1e-05
rope_base = 100000000000.0
negative = -1e30


def shifted(block, axis, distance):
    devices = range(lax.axis_size(axis))
    route = [(i - distance, i) for i in devices if i - distance in devices]
    return lax.ppermute(block, axis, route)


def prefix(part, axis, combine, identity):
    place = lax.axis_index(axis)
    gathered = jax.tree.map(lambda a: lax.all_gather(a, axis), part)
    state = jax.tree.map(lambda a, e: jnp.zeros_like(a) + jnp.asarray(e, a.dtype), part, identity)

    def one(turn, state):
        return combine(
            state, jax.tree.map(lambda a: lax.dynamic_index_in_dim(a, turn, 0, False), gathered)
        )

    return lax.fori_loop(0, place, one, state)


def attend(query_rows, query_rank, pieces, key_rank, block):
    rows = query_rows.shape[0]
    count = pieces.shape[0]
    steps = count // block
    scale = 1.0 / float(HD) ** 0.5

    def kernel(qr_ref, q_ref, kr_ref, kv_ref, out_ref, top_ref, total_ref, acc_ref):
        step = pl.program_id(0)

        @pl.when(step == 0)
        def _():
            top_ref[...] = jnp.full(top_ref.shape, negative, jnp.float32)
            total_ref[...] = jnp.zeros(total_ref.shape, jnp.float32)
            acc_ref[...] = jnp.zeros(acc_ref.shape, jnp.float32)

        scores = lax.dot_general(
            q_ref[...], kv_ref[:, :HD], (((1,), (1,)), ((), ())), preferred_element_type=jnp.float32
        ) * scale
        valid = kr_ref[...] <= qr_ref[...]
        masked = jnp.where(valid, scores, negative)
        old = top_ref[...]
        new = jnp.maximum(old, jnp.max(masked, axis=1, keepdims=True))
        weights = jnp.where(valid, jnp.exp(masked - new), 0.0)
        alpha = jnp.exp(old - new)
        total_ref[...] = alpha * total_ref[...] + jnp.sum(weights, axis=1, keepdims=True)
        acc_ref[...] = alpha * acc_ref[...] + jnp.dot(
            weights.astype(jnp.bfloat16), kv_ref[:, HD:], preferred_element_type=jnp.float32
        )
        top_ref[...] = new

        @pl.when(step == steps - 1)
        def _():
            out_ref[...] = (acc_ref[...] / total_ref[...]).astype(out_ref.dtype)

    return pl.pallas_call(
        kernel,
        grid=(steps,),
        in_specs=[
            pl.BlockSpec((rows, 1), lambda i: (0, 0)),
            pl.BlockSpec((rows, HD), lambda i: (0, 0)),
            pl.BlockSpec((1, block), lambda i: (0, i)),
            pl.BlockSpec((block, 2 * HD), lambda i: (i, 0)),
        ],
        out_specs=pl.BlockSpec((rows, HD), lambda i: (0, 0)),
        out_shape=jax.ShapeDtypeStruct((rows, HD), jnp.bfloat16),
        scratch_shapes=[
            pltpu.VMEM((rows, 1), jnp.float32),
            pltpu.VMEM((rows, 1), jnp.float32),
            pltpu.VMEM((rows, HD), jnp.float32),
        ],
        compiler_params=pltpu.CompilerParams(vmem_limit_bytes=48 * 1024 * 1024),
    )(query_rank, query_rows, key_rank, pieces)


def rotate(values, positions):
    half = HD // 2
    freqs = rope_base ** (-jnp.arange(half, dtype=jnp.float32) * 2.0 / HD)
    angles = positions.astype(jnp.float32)[:, None] * freqs[None, :]
    cosine = jnp.cos(angles)[:, None, :]
    sine = jnp.sin(angles)[:, None, :]
    first = values[..., :half]
    second = values[..., half:]
    return jnp.concatenate(
        [first * cosine - second * sine, second * cosine + first * sine], axis=-1
    )


def rms_scale(values):
    mean_sq = jnp.mean(values * values, axis=-1, keepdims=True)
    return values * lax.rsqrt(mean_sq + epsilon)


def causal_conv(tail, inputs, taps):
    padded = jnp.concatenate([tail, inputs], axis=0).astype(jnp.float32)
    count = inputs.shape[0]
    total = jnp.zeros(inputs.shape, jnp.float32)
    for offset in range(CONV):
        total = total + taps[offset].astype(jnp.float32)[None, :] * padded[offset : offset + count]
    return jax.nn.silu(total)


def join_states(earlier, later):
    return (earlier[0] * later[0], later[0][:, None, None] * earlier[1] + later[1])


def shards(
    hidden,
    norm_gain,
    w_query,
    w_keyval,
    w_attn_out,
    w_inner,
    w_bc,
    w_dt,
    dt_bias,
    a_log,
    d_skip,
    conv_x,
    conv_bc,
    mamba_gain,
    w_mamba_out,
    cache,
    cache_len,
    tail_x,
    tail_bc,
    ssm_init,
):
    high = lax.Precision.HIGHEST
    own_rows = hidden[0]
    tokens = own_rows.shape[0]
    seq_pos = lax.axis_index("seq")
    mp_pos = lax.axis_index("mp")
    length = cache_len[0]
    mp_count = lax.axis_size("mp")
    width = own_rows.shape[1]
    whole = jnp.zeros((tokens, mp_count * width), own_rows.dtype)
    for shift in range(mp_count):
        if shift == 0:
            part = own_rows
        else:
            part = lax.ppermute(own_rows, "mp", [(i, (i + shift) % mp_count) for i in range(mp_count)])
        source = (lax.axis_index("mp") + mp_count - shift) % mp_count
        whole = lax.dynamic_update_slice(whole, part, (0, source * width))
    normed = (rms_scale(whole.astype(jnp.float32)) * norm_gain.astype(jnp.float32)).astype(
        jnp.bfloat16
    )
    positions = length + seq_pos * tokens + jnp.arange(tokens, dtype=jnp.int32)
    local_heads = w_query.shape[1] // HD
    query = rotate(
        jnp.dot(normed, w_query, preferred_element_type=jnp.float32).reshape(
            tokens, local_heads, HD
        ),
        positions,
    ).astype(jnp.bfloat16)
    mp_size = lax.axis_size("mp")
    pairs_of = [(i, i ^ 1) for i in range(mp_size)]
    is_key_block = mp_pos % 2 == 0

    def paired(own):
        other = lax.ppermute(own, "mp", pairs_of)
        return jnp.where(
            is_key_block,
            jnp.concatenate([own, other], axis=1),
            jnp.concatenate([other, own], axis=1),
        )

    cache_pair = paired(cache[0])
    projected = jnp.dot(normed, paired(w_keyval), preferred_element_type=jnp.float32)
    roped = rotate(projected[:, None, :HD], positions)[:, 0, :]
    kv_pair = jnp.concatenate([roped, projected[:, HD:]], axis=1).astype(jnp.bfloat16)
    kv_block = jnp.where(is_key_block, kv_pair[:, :HD], kv_pair[:, HD:])
    group_rows = jnp.concatenate([cache_pair, kv_pair], axis=0)
    bc_block = jnp.dot(normed, w_bc, preferred_element_type=jnp.float32).astype(jnp.bfloat16)
    bc_all = lax.all_gather(bc_block, "mp", axis=1, tiled=True)
    inner = jnp.einsum("td,dkc->tkc", normed, w_inner, preferred_element_type=jnp.float32).astype(
        jnp.bfloat16
    )
    rim = CONV - 1
    prev_x, prev_bc = shifted((inner[tokens - rim :, 1], bc_all[tokens - rim :]), "seq", 1)
    first_block = seq_pos == 0
    prev_x = jnp.where(first_block, tail_x[0], prev_x)
    prev_bc = jnp.where(first_block, tail_bc[0], prev_bc)
    mamba_heads = dt_bias.shape[0]
    x_conv = causal_conv(prev_x, inner[:, 1], conv_x).reshape(tokens, mamba_heads, HD)
    bc_conv = causal_conv(prev_bc, bc_all, conv_bc)
    b_mat = bc_conv[:, :NS]
    c_mat = bc_conv[:, NS:]
    step_size = jax.nn.softplus(jnp.dot(normed, w_dt, preferred_element_type=jnp.float32) + dt_bias)
    log_decay = -step_size * jnp.exp(a_log)[None, :]
    cumulative = jnp.cumsum(log_decay, axis=0)
    pairs = jnp.dot(c_mat, b_mat.T, precision=high)
    gap = cumulative[:, None, :] - cumulative[None, :, :]
    token_ids = jnp.arange(tokens)
    lower = (token_ids[:, None] >= token_ids[None, :])[:, :, None]
    decay = jnp.where(lower, jnp.exp(jnp.where(lower, gap, 0.0)), 0.0)
    mixing = decay * pairs[:, :, None] * step_size[None, :, :]
    inner_out = jnp.einsum("tsh,shp->thp", mixing, x_conv, precision=high)
    to_end = jnp.exp(cumulative[-1][None, :] - cumulative) * step_size
    own_state = jnp.einsum("sh,shp,sn->hpn", to_end, x_conv, b_mat, precision=high)
    block_decay = jnp.exp(cumulative[-1])
    seq_size = lax.axis_size("seq")
    rows = HD // seq_size
    pieces = jnp.transpose(own_state.reshape(mamba_heads, seq_size, rows, NS), (1, 0, 2, 3))
    decays = jnp.broadcast_to(block_decay[None, :, None, None], (seq_size, mamba_heads, 1, NS))
    columns = lax.all_to_all(jnp.concatenate([pieces, decays], axis=2), "seq", 0, 0, tiled=True)
    carry = lax.dynamic_slice_in_dim(ssm_init[0], seq_pos * rows, rows, 1)
    entering = []
    for source in range(seq_size):
        entering.append(carry)
        part = columns[source]
        carry = part[:, rows:, :] * carry + part[:, :rows, :]
    entering = lax.all_to_all(jnp.stack(entering, axis=0), "seq", 0, 0, tiled=True)
    incoming = jnp.transpose(entering, (1, 0, 2, 3)).reshape(mamba_heads, HD, NS)
    carried = jnp.exp(cumulative)[:, :, None] * jnp.einsum(
        "tn,hpn->thp", c_mat, incoming, precision=high
    )
    mamba_y = inner_out + carried + d_skip[None, :, None] * x_conv
    state_after = block_decay[:, None, None] * incoming + own_state
    gated = mamba_y * jax.nn.silu(inner[:, 0].astype(jnp.float32).reshape(tokens, mamba_heads, HD))
    mixed = (
        rms_scale(gated).reshape(tokens, mamba_heads * HD) * mamba_gain.astype(jnp.float32)
    ).astype(jnp.bfloat16)
    cache_rows = cache.shape[1]
    shard_rows = cache_rows + tokens
    group = mp_pos * local_heads // (QH // KVH)
    query_index = seq_pos * tokens + jnp.arange(tokens, dtype=jnp.int32)
    scale = 1.0 / float(HD) ** 0.5
    piece = lax.all_gather(group_rows, "seq", axis=0, tiled=True)
    count = piece.shape[0]
    index = jnp.arange(count, dtype=jnp.int32)
    owner = index // shard_rows
    offset = index % shard_rows
    in_cache = offset < cache_rows
    slot_ok = in_cache & (owner * cache_rows + offset < length)
    new_index = owner * tokens + offset - cache_rows
    never = jnp.iinfo(jnp.int32).max
    key_rank = jnp.where(in_cache, jnp.where(slot_ok, -1, never), new_index)[None, :]
    query_rank = jnp.tile(query_index, local_heads)[:, None]
    query_rows = jnp.transpose(query, (1, 0, 2)).reshape(local_heads * tokens, HD)
    attended = attend(query_rows, query_rank, piece, key_rank, 4 * shard_rows)
    attended = jnp.transpose(attended.reshape(local_heads, tokens, HD), (1, 0, 2)).reshape(
        tokens, local_heads * HD
    )
    attended = attended.astype(jnp.bfloat16)
    term = jnp.dot(attended, w_attn_out, preferred_element_type=jnp.float32)
    term = term + jnp.dot(mixed, w_mamba_out, preferred_element_type=jnp.float32)
    summed = lax.psum_scatter(term.astype(jnp.bfloat16), "mp", scatter_dimension=1, tiled=True)
    summed = summed.astype(jnp.float32)
    layer = (summed + own_rows.astype(jnp.float32)).astype(jnp.bfloat16)
    return (layer[None], kv_block[None], state_after[None, None])


def solution(mesh):
    placed = (
        P("req", "seq", "mp"),
        P(),
        P(None, "mp"),
        P(None, "mp"),
        P("mp", None),
        P(None, None, "mp"),
        P(None, "mp"),
        P(None, "mp"),
        P("mp"),
        P("mp"),
        P("mp"),
        P(None, "mp"),
        P(),
        P("mp"),
        P("mp", None),
        P("req", "seq", "mp"),
        P("req"),
        P("req", None, "mp"),
        P("req", None, None),
        P("req", "mp", None, None),
    )
    return jax.shard_map(
        shards,
        mesh=mesh,
        in_specs=placed,
        out_specs=(P("req", "seq", "mp"), P("req", "seq", "mp"), P("req", "seq", "mp", None, None)),
        check_vma=False,
    )
```

```python
import jax
import jax.numpy as jnp
from jax import lax
from jax.sharding import PartitionSpec as P
from jax.experimental import pallas as pl
from jax.experimental.pallas import tpu as pltpu

HD = 128
QH = 8
KVH = 2
NS = 256
CONV = 4


epsilon = 1e-05
rope_base = 100000000000.0
negative = -1e30


def shifted(block, axis, distance):
    devices = range(lax.axis_size(axis))
    route = [(i - distance, i) for i in devices if i - distance in devices]
    return lax.ppermute(block, axis, route)


def prefix(part, axis, combine, identity):
    place = lax.axis_index(axis)
    gathered = jax.tree.map(lambda a: lax.all_gather(a, axis), part)
    state = jax.tree.map(lambda a, e: jnp.zeros_like(a) + jnp.asarray(e, a.dtype), part, identity)

    def one(turn, state):
        return combine(
            state, jax.tree.map(lambda a: lax.dynamic_index_in_dim(a, turn, 0, False), gathered)
        )

    return lax.fori_loop(0, place, one, state)


def attend(query_rows, query_rank, pieces, key_rank, block):
    rows = query_rows.shape[0]
    count = pieces.shape[0]
    steps = count // block
    scale = 1.0 / float(HD) ** 0.5

    def kernel(qr_ref, q_ref, kr_ref, kv_ref, out_ref, top_ref, total_ref, acc_ref):
        step = pl.program_id(0)

        @pl.when(step == 0)
        def _():
            top_ref[...] = jnp.full(top_ref.shape, negative, jnp.float32)
            total_ref[...] = jnp.zeros(total_ref.shape, jnp.float32)
            acc_ref[...] = jnp.zeros(acc_ref.shape, jnp.float32)

        scores = lax.dot_general(
            q_ref[...], kv_ref[:, :HD], (((1,), (1,)), ((), ())), preferred_element_type=jnp.float32
        ) * scale
        valid = kr_ref[...] <= qr_ref[...]
        masked = jnp.where(valid, scores, negative)
        old = top_ref[...]
        new = jnp.maximum(old, jnp.max(masked, axis=1, keepdims=True))
        weights = jnp.where(valid, jnp.exp(masked - new), 0.0)
        alpha = jnp.exp(old - new)
        total_ref[...] = alpha * total_ref[...] + jnp.sum(weights, axis=1, keepdims=True)
        acc_ref[...] = alpha * acc_ref[...] + jnp.dot(
            weights.astype(jnp.bfloat16), kv_ref[:, HD:], preferred_element_type=jnp.float32
        )
        top_ref[...] = new

        @pl.when(step == steps - 1)
        def _():
            out_ref[...] = (acc_ref[...] / total_ref[...]).astype(out_ref.dtype)

    return pl.pallas_call(
        kernel,
        grid=(steps,),
        in_specs=[
            pl.BlockSpec((rows, 1), lambda i: (0, 0)),
            pl.BlockSpec((rows, HD), lambda i: (0, 0)),
            pl.BlockSpec((1, block), lambda i: (0, i)),
            pl.BlockSpec((block, 2 * HD), lambda i: (i, 0)),
        ],
        out_specs=pl.BlockSpec((rows, HD), lambda i: (0, 0)),
        out_shape=jax.ShapeDtypeStruct((rows, HD), jnp.bfloat16),
        scratch_shapes=[
            pltpu.VMEM((rows, 1), jnp.float32),
            pltpu.VMEM((rows, 1), jnp.float32),
            pltpu.VMEM((rows, HD), jnp.float32),
        ],
        compiler_params=pltpu.CompilerParams(vmem_limit_bytes=48 * 1024 * 1024),
    )(query_rank, query_rows, key_rank, pieces)


def rotate(values, positions):
    half = HD // 2
    freqs = rope_base ** (-jnp.arange(half, dtype=jnp.float32) * 2.0 / HD)
    angles = positions.astype(jnp.float32)[:, None] * freqs[None, :]
    cosine = jnp.cos(angles)[:, None, :]
    sine = jnp.sin(angles)[:, None, :]
    first = values[..., :half]
    second = values[..., half:]
    return jnp.concatenate(
        [first * cosine - second * sine, second * cosine + first * sine], axis=-1
    )


def rms_scale(values):
    mean_sq = jnp.mean(values * values, axis=-1, keepdims=True)
    return values * lax.rsqrt(mean_sq + epsilon)


def causal_conv(tail, inputs, taps):
    padded = jnp.concatenate([tail, inputs], axis=0).astype(jnp.float32)
    count = inputs.shape[0]
    total = jnp.zeros(inputs.shape, jnp.float32)
    for offset in range(CONV):
        total = total + taps[offset].astype(jnp.float32)[None, :] * padded[offset : offset + count]
    return jax.nn.silu(total)


def join_states(earlier, later):
    return (earlier[0] * later[0], later[0][:, None, None] * earlier[1] + later[1])


def shards(
    hidden,
    norm_gain,
    w_query,
    w_keyval,
    w_attn_out,
    w_inner,
    w_bc,
    w_dt,
    dt_bias,
    a_log,
    d_skip,
    conv_x,
    conv_bc,
    mamba_gain,
    w_mamba_out,
    cache,
    cache_len,
    tail_x,
    tail_bc,
    ssm_init,
):
    high = lax.Precision.HIGHEST
    own_rows = hidden[0]
    tokens = own_rows.shape[0]
    seq_pos = lax.axis_index("seq")
    mp_pos = lax.axis_index("mp")
    length = cache_len[0]
    mp_count = lax.axis_size("mp")
    width = own_rows.shape[1]
    whole = jnp.zeros((tokens, mp_count * width), own_rows.dtype)
    for shift in range(mp_count):
        if shift == 0:
            part = own_rows
        else:
            part = lax.ppermute(own_rows, "mp", [(i, (i + shift) % mp_count) for i in range(mp_count)])
        source = (lax.axis_index("mp") + mp_count - shift) % mp_count
        whole = lax.dynamic_update_slice(whole, part, (0, source * width))
    normed = (rms_scale(whole.astype(jnp.float32)) * norm_gain.astype(jnp.float32)).astype(
        jnp.bfloat16
    )
    positions = length + seq_pos * tokens + jnp.arange(tokens, dtype=jnp.int32)
    local_heads = w_query.shape[1] // HD
    query = rotate(
        jnp.dot(normed, w_query, preferred_element_type=jnp.float32).reshape(
            tokens, local_heads, HD
        ),
        positions,
    ).astype(jnp.bfloat16)
    projected = jnp.dot(normed, w_keyval, preferred_element_type=jnp.float32)
    roped = rotate(projected[:, None, :], positions)[:, 0, :]
    kv_block = jnp.where(mp_pos % 2 == 0, roped, projected).astype(jnp.bfloat16)
    bc_block = jnp.dot(normed, w_bc, preferred_element_type=jnp.float32).astype(jnp.bfloat16)
    bc_all = lax.all_gather(bc_block, "mp", axis=1, tiled=True)
    own_rows_kv = jnp.concatenate([cache[0], kv_block], axis=0)
    mp_size = lax.axis_size("mp")
    partner = lax.ppermute(own_rows_kv, "mp", [(i, i ^ 1) for i in range(mp_size)])
    is_key_block = mp_pos % 2 == 0
    group_rows = jnp.where(
        is_key_block,
        jnp.concatenate([own_rows_kv, partner], axis=1),
        jnp.concatenate([partner, own_rows_kv], axis=1),
    )
    inner = jnp.einsum("td,dkc->tkc", normed, w_inner, preferred_element_type=jnp.float32).astype(
        jnp.bfloat16
    )
    rim = CONV - 1
    prev_x, prev_bc = shifted((inner[tokens - rim :, 1], bc_all[tokens - rim :]), "seq", 1)
    first_block = seq_pos == 0
    prev_x = jnp.where(first_block, tail_x[0], prev_x)
    prev_bc = jnp.where(first_block, tail_bc[0], prev_bc)
    mamba_heads = dt_bias.shape[0]
    x_conv = causal_conv(prev_x, inner[:, 1], conv_x).reshape(tokens, mamba_heads, HD)
    bc_conv = causal_conv(prev_bc, bc_all, conv_bc)
    b_mat = bc_conv[:, :NS]
    c_mat = bc_conv[:, NS:]
    step_size = jax.nn.softplus(jnp.dot(normed, w_dt, preferred_element_type=jnp.float32) + dt_bias)
    log_decay = -step_size * jnp.exp(a_log)[None, :]
    cumulative = jnp.cumsum(log_decay, axis=0)
    pairs = jnp.dot(c_mat, b_mat.T, precision=high)
    gap = cumulative[:, None, :] - cumulative[None, :, :]
    token_ids = jnp.arange(tokens)
    lower = (token_ids[:, None] >= token_ids[None, :])[:, :, None]
    decay = jnp.where(lower, jnp.exp(jnp.where(lower, gap, 0.0)), 0.0)
    mixing = decay * pairs[:, :, None] * step_size[None, :, :]
    inner_out = jnp.einsum("tsh,shp->thp", mixing, x_conv, precision=high)
    to_end = jnp.exp(cumulative[-1][None, :] - cumulative) * step_size
    own_state = jnp.einsum("sh,shp,sn->hpn", to_end, x_conv, b_mat, precision=high)
    block_decay = jnp.exp(cumulative[-1])
    seq_size = lax.axis_size("seq")
    rows = HD // seq_size
    pieces = jnp.transpose(own_state.reshape(mamba_heads, seq_size, rows, NS), (1, 0, 2, 3))
    decays = jnp.broadcast_to(block_decay[None, :, None, None], (seq_size, mamba_heads, 1, NS))
    columns = lax.all_to_all(jnp.concatenate([pieces, decays], axis=2), "seq", 0, 0, tiled=True)
    carry = lax.dynamic_slice_in_dim(ssm_init[0], seq_pos * rows, rows, 1)
    entering = []
    for source in range(seq_size):
        entering.append(carry)
        part = columns[source]
        carry = part[:, rows:, :] * carry + part[:, :rows, :]
    entering = lax.all_to_all(jnp.stack(entering, axis=0), "seq", 0, 0, tiled=True)
    incoming = jnp.transpose(entering, (1, 0, 2, 3)).reshape(mamba_heads, HD, NS)
    carried = jnp.exp(cumulative)[:, :, None] * jnp.einsum(
        "tn,hpn->thp", c_mat, incoming, precision=high
    )
    mamba_y = inner_out + carried + d_skip[None, :, None] * x_conv
    state_after = block_decay[:, None, None] * incoming + own_state
    gated = mamba_y * jax.nn.silu(inner[:, 0].astype(jnp.float32).reshape(tokens, mamba_heads, HD))
    mixed = (
        rms_scale(gated).reshape(tokens, mamba_heads * HD) * mamba_gain.astype(jnp.float32)
    ).astype(jnp.bfloat16)
    cache_rows = cache.shape[1]
    shard_rows = cache_rows + tokens
    group = mp_pos * local_heads // (QH // KVH)
    query_index = seq_pos * tokens + jnp.arange(tokens, dtype=jnp.int32)
    scale = 1.0 / float(HD) ** 0.5
    piece = lax.all_gather(group_rows, "seq", axis=0, tiled=True)
    count = piece.shape[0]
    index = jnp.arange(count, dtype=jnp.int32)
    owner = index // shard_rows
    offset = index % shard_rows
    in_cache = offset < cache_rows
    slot_ok = in_cache & (owner * cache_rows + offset < length)
    new_index = owner * tokens + offset - cache_rows
    never = jnp.iinfo(jnp.int32).max
    key_rank = jnp.where(in_cache, jnp.where(slot_ok, -1, never), new_index)[None, :]
    query_rank = jnp.tile(query_index, local_heads)[:, None]
    query_rows = jnp.transpose(query, (1, 0, 2)).reshape(local_heads * tokens, HD)
    attended = attend(query_rows, query_rank, piece, key_rank, 8 * shard_rows)
    attended = jnp.transpose(attended.reshape(local_heads, tokens, HD), (1, 0, 2)).reshape(
        tokens, local_heads * HD
    )
    attended = attended.astype(jnp.bfloat16)
    term = jnp.dot(attended, w_attn_out, preferred_element_type=jnp.float32)
    term = term + jnp.dot(mixed, w_mamba_out, preferred_element_type=jnp.float32)
    summed = lax.psum_scatter(term.astype(jnp.bfloat16), "mp", scatter_dimension=1, tiled=True)
    summed = summed.astype(jnp.float32)
    layer = (summed + own_rows.astype(jnp.float32)).astype(jnp.bfloat16)
    return (layer[None], kv_block[None], state_after[None, None])


def solution(mesh):
    placed = (
        P("req", "seq", "mp"),
        P(),
        P(None, "mp"),
        P(None, "mp"),
        P("mp", None),
        P(None, None, "mp"),
        P(None, "mp"),
        P(None, "mp"),
        P("mp"),
        P("mp"),
        P("mp"),
        P(None, "mp"),
        P(),
        P("mp"),
        P("mp", None),
        P("req", "seq", "mp"),
        P("req"),
        P("req", None, "mp"),
        P("req", None, None),
        P("req", "mp", None, None),
    )
    return jax.shard_map(
        shards,
        mesh=mesh,
        in_specs=placed,
        out_specs=(P("req", "seq", "mp"), P("req", "seq", "mp"), P("req", "seq", "mp", None, None)),
        check_vma=False,
    )
```

```python
import jax
import jax.numpy as jnp
from jax import lax
from jax.sharding import PartitionSpec as P
from jax.experimental import pallas as pl
from jax.experimental.pallas import tpu as pltpu

HD = 128
QH = 8
KVH = 2
NS = 256
CONV = 4


epsilon = 1e-05
rope_base = 100000000000.0
negative = -1e30


def shifted(block, axis, distance):
    devices = range(lax.axis_size(axis))
    route = [(i - distance, i) for i in devices if i - distance in devices]
    return lax.ppermute(block, axis, route)


def prefix(part, axis, combine, identity):
    place = lax.axis_index(axis)
    gathered = jax.tree.map(lambda a: lax.all_gather(a, axis), part)
    state = jax.tree.map(lambda a, e: jnp.zeros_like(a) + jnp.asarray(e, a.dtype), part, identity)

    def one(turn, state):
        return combine(
            state, jax.tree.map(lambda a: lax.dynamic_index_in_dim(a, turn, 0, False), gathered)
        )

    return lax.fori_loop(0, place, one, state)


def attend(query_rows, query_rank, pieces, key_rank, block):
    rows = query_rows.shape[0]
    count = pieces.shape[0]
    steps = count // block
    scale = 1.0 / float(HD) ** 0.5

    def kernel(qr_ref, q_ref, kr_ref, kv_ref, out_ref, top_ref, total_ref, acc_ref):
        step = pl.program_id(0)

        @pl.when(step == 0)
        def _():
            top_ref[...] = jnp.full(top_ref.shape, negative, jnp.float32)
            total_ref[...] = jnp.zeros(total_ref.shape, jnp.float32)
            acc_ref[...] = jnp.zeros(acc_ref.shape, jnp.float32)

        scores = lax.dot_general(
            q_ref[...], kv_ref[:, :HD], (((1,), (1,)), ((), ())), preferred_element_type=jnp.float32
        ) * scale
        valid = kr_ref[...] <= qr_ref[...]
        masked = jnp.where(valid, scores, negative)
        old = top_ref[...]
        new = jnp.maximum(old, jnp.max(masked, axis=1, keepdims=True))
        weights = jnp.where(valid, jnp.exp(masked - new), 0.0)
        alpha = jnp.exp(old - new)
        total_ref[...] = alpha * total_ref[...] + jnp.sum(weights, axis=1, keepdims=True)
        acc_ref[...] = alpha * acc_ref[...] + jnp.dot(
            weights.astype(jnp.bfloat16), kv_ref[:, HD:], preferred_element_type=jnp.float32
        )
        top_ref[...] = new

        @pl.when(step == steps - 1)
        def _():
            out_ref[...] = (acc_ref[...] / total_ref[...]).astype(out_ref.dtype)

    return pl.pallas_call(
        kernel,
        grid=(steps,),
        in_specs=[
            pl.BlockSpec((rows, 1), lambda i: (0, 0)),
            pl.BlockSpec((rows, HD), lambda i: (0, 0)),
            pl.BlockSpec((1, block), lambda i: (0, i)),
            pl.BlockSpec((block, 2 * HD), lambda i: (i, 0)),
        ],
        out_specs=pl.BlockSpec((rows, HD), lambda i: (0, 0)),
        out_shape=jax.ShapeDtypeStruct((rows, HD), jnp.bfloat16),
        scratch_shapes=[
            pltpu.VMEM((rows, 1), jnp.float32),
            pltpu.VMEM((rows, 1), jnp.float32),
            pltpu.VMEM((rows, HD), jnp.float32),
        ],
        compiler_params=pltpu.CompilerParams(vmem_limit_bytes=48 * 1024 * 1024),
    )(query_rank, query_rows, key_rank, pieces)


def rotate(values, positions):
    half = HD // 2
    freqs = rope_base ** (-jnp.arange(half, dtype=jnp.float32) * 2.0 / HD)
    angles = positions.astype(jnp.float32)[:, None] * freqs[None, :]
    cosine = jnp.cos(angles)[:, None, :]
    sine = jnp.sin(angles)[:, None, :]
    first = values[..., :half]
    second = values[..., half:]
    return jnp.concatenate(
        [first * cosine - second * sine, second * cosine + first * sine], axis=-1
    )


def rms_scale(values):
    mean_sq = jnp.mean(values * values, axis=-1, keepdims=True)
    return values * lax.rsqrt(mean_sq + epsilon)


def causal_conv(tail, inputs, taps):
    padded = jnp.concatenate([tail, inputs], axis=0).astype(jnp.float32)
    count = inputs.shape[0]
    total = jnp.zeros(inputs.shape, jnp.float32)
    for offset in range(CONV):
        total = total + taps[offset].astype(jnp.float32)[None, :] * padded[offset : offset + count]
    return jax.nn.silu(total)


def join_states(earlier, later):
    return (earlier[0] * later[0], later[0][:, None, None] * earlier[1] + later[1])


def shards(
    hidden,
    norm_gain,
    w_query,
    w_keyval,
    w_attn_out,
    w_inner,
    w_bc,
    w_dt,
    dt_bias,
    a_log,
    d_skip,
    conv_x,
    conv_bc,
    mamba_gain,
    w_mamba_out,
    cache,
    cache_len,
    tail_x,
    tail_bc,
    ssm_init,
):
    high = lax.Precision.HIGHEST
    own_rows = hidden[0]
    tokens = own_rows.shape[0]
    seq_pos = lax.axis_index("seq")
    mp_pos = lax.axis_index("mp")
    length = cache_len[0]
    mp_count = lax.axis_size("mp")
    width = own_rows.shape[1]
    whole = jnp.zeros((tokens, mp_count * width), own_rows.dtype)
    for shift in range(mp_count):
        if shift == 0:
            part = own_rows
        else:
            part = lax.ppermute(own_rows, "mp", [(i, (i + shift) % mp_count) for i in range(mp_count)])
        source = (lax.axis_index("mp") + mp_count - shift) % mp_count
        whole = lax.dynamic_update_slice(whole, part, (0, source * width))
    normed = (rms_scale(whole.astype(jnp.float32)) * norm_gain.astype(jnp.float32)).astype(
        jnp.bfloat16
    )
    positions = length + seq_pos * tokens + jnp.arange(tokens, dtype=jnp.int32)
    local_heads = w_query.shape[1] // HD
    query = rotate(
        jnp.dot(normed, w_query, preferred_element_type=jnp.float32).reshape(
            tokens, local_heads, HD
        ),
        positions,
    ).astype(jnp.bfloat16)
    projected = jnp.dot(normed, w_keyval, preferred_element_type=jnp.float32)
    roped = rotate(projected[:, None, :], positions)[:, 0, :]
    kv_block = jnp.where(mp_pos % 2 == 0, roped, projected).astype(jnp.bfloat16)
    bc_block = jnp.dot(normed, w_bc, preferred_element_type=jnp.float32).astype(jnp.bfloat16)
    bc_all = lax.all_gather(bc_block, "mp", axis=1, tiled=True)
    own_rows_kv = jnp.concatenate([cache[0], kv_block], axis=0)
    mp_size = lax.axis_size("mp")
    partner = lax.ppermute(own_rows_kv, "mp", [(i, i ^ 1) for i in range(mp_size)])
    is_key_block = mp_pos % 2 == 0
    group_rows = jnp.where(
        is_key_block,
        jnp.concatenate([own_rows_kv, partner], axis=1),
        jnp.concatenate([partner, own_rows_kv], axis=1),
    )
    inner = jnp.einsum("td,dkc->tkc", normed, w_inner, preferred_element_type=jnp.float32).astype(
        jnp.bfloat16
    )
    rim = CONV - 1
    prev_x, prev_bc = shifted((inner[tokens - rim :, 1], bc_all[tokens - rim :]), "seq", 1)
    first_block = seq_pos == 0
    prev_x = jnp.where(first_block, tail_x[0], prev_x)
    prev_bc = jnp.where(first_block, tail_bc[0], prev_bc)
    mamba_heads = dt_bias.shape[0]
    x_conv = causal_conv(prev_x, inner[:, 1], conv_x).reshape(tokens, mamba_heads, HD)
    bc_conv = causal_conv(prev_bc, bc_all, conv_bc)
    b_mat = bc_conv[:, :NS]
    c_mat = bc_conv[:, NS:]
    step_size = jax.nn.softplus(jnp.dot(normed, w_dt, preferred_element_type=jnp.float32) + dt_bias)
    log_decay = -step_size * jnp.exp(a_log)[None, :]
    cumulative = jnp.cumsum(log_decay, axis=0)
    pairs = jnp.dot(c_mat, b_mat.T, precision=high)
    gap = cumulative[:, None, :] - cumulative[None, :, :]
    token_ids = jnp.arange(tokens)
    lower = (token_ids[:, None] >= token_ids[None, :])[:, :, None]
    decay = jnp.where(lower, jnp.exp(jnp.where(lower, gap, 0.0)), 0.0)
    mixing = decay * pairs[:, :, None] * step_size[None, :, :]
    inner_out = jnp.einsum("tsh,shp->thp", mixing, x_conv, precision=high)
    to_end = jnp.exp(cumulative[-1][None, :] - cumulative) * step_size
    own_state = jnp.einsum("sh,shp,sn->hpn", to_end, x_conv, b_mat, precision=high)
    block_decay = jnp.exp(cumulative[-1])
    seq_size = lax.axis_size("seq")
    rows = HD // seq_size
    pieces = jnp.transpose(own_state.reshape(mamba_heads, seq_size, rows, NS), (1, 0, 2, 3))
    decays = jnp.broadcast_to(block_decay[None, :, None, None], (seq_size, mamba_heads, 1, NS))
    columns = lax.all_to_all(jnp.concatenate([pieces, decays], axis=2), "seq", 0, 0, tiled=True)
    carry = lax.dynamic_slice_in_dim(ssm_init[0], seq_pos * rows, rows, 1)
    entering = []
    for source in range(seq_size):
        entering.append(carry)
        part = columns[source]
        carry = part[:, rows:, :] * carry + part[:, :rows, :]
    entering = lax.all_to_all(jnp.stack(entering, axis=0), "seq", 0, 0, tiled=True)
    incoming = jnp.transpose(entering, (1, 0, 2, 3)).reshape(mamba_heads, HD, NS)
    carried = jnp.exp(cumulative)[:, :, None] * jnp.einsum(
        "tn,hpn->thp", c_mat, incoming, precision=high
    )
    mamba_y = inner_out + carried + d_skip[None, :, None] * x_conv
    state_after = block_decay[:, None, None] * incoming + own_state
    gated = mamba_y * jax.nn.silu(inner[:, 0].astype(jnp.float32).reshape(tokens, mamba_heads, HD))
    mixed = (
        rms_scale(gated).reshape(tokens, mamba_heads * HD) * mamba_gain.astype(jnp.float32)
    ).astype(jnp.bfloat16)
    cache_rows = cache.shape[1]
    shard_rows = cache_rows + tokens
    group = mp_pos * local_heads // (QH // KVH)
    query_index = seq_pos * tokens + jnp.arange(tokens, dtype=jnp.int32)
    scale = 1.0 / float(HD) ** 0.5
    piece = lax.all_gather(group_rows, "seq", axis=0, tiled=True)
    count = piece.shape[0]
    index = jnp.arange(count, dtype=jnp.int32)
    owner = index // shard_rows
    offset = index % shard_rows
    in_cache = offset < cache_rows
    slot_ok = in_cache & (owner * cache_rows + offset < length)
    new_index = owner * tokens + offset - cache_rows
    never = jnp.iinfo(jnp.int32).max
    key_rank = jnp.where(in_cache, jnp.where(slot_ok, -1, never), new_index)[None, :]
    query_rank = jnp.tile(query_index, local_heads)[:, None]
    query_rows = jnp.transpose(query, (1, 0, 2)).reshape(local_heads * tokens, HD)
    attended = attend(query_rows, query_rank, piece, key_rank, 8 * shard_rows)
    attended = jnp.transpose(attended.reshape(local_heads, tokens, HD), (1, 0, 2)).reshape(
        tokens, local_heads * HD
    )
    attended = attended.astype(jnp.bfloat16)
    mp_count = lax.axis_size("mp")
    out_cols = w_attn_out.shape[1] // mp_count
    attn_cols = lax.all_to_all(
        w_attn_out.reshape(w_attn_out.shape[0], mp_count, out_cols), "mp", 1, 0, tiled=True
    ).reshape(w_attn_out.shape[0] * mp_count, out_cols)
    mamba_term = jnp.dot(mixed, w_mamba_out, preferred_element_type=jnp.float32)
    summed = lax.psum_scatter(mamba_term.astype(jnp.bfloat16), "mp", scatter_dimension=1, tiled=True)
    attended_all = lax.all_gather(attended, "mp", axis=1, tiled=True)
    summed = summed.astype(jnp.float32) + jnp.dot(
        attended_all, attn_cols, preferred_element_type=jnp.float32
    )
    layer = (summed + own_rows.astype(jnp.float32)).astype(jnp.bfloat16)
    return (layer[None], kv_block[None], state_after[None, None])


def solution(mesh):
    placed = (
        P("req", "seq", "mp"),
        P(),
        P(None, "mp"),
        P(None, "mp"),
        P("mp", None),
        P(None, None, "mp"),
        P(None, "mp"),
        P(None, "mp"),
        P("mp"),
        P("mp"),
        P("mp"),
        P(None, "mp"),
        P(),
        P("mp"),
        P("mp", None),
        P("req", "seq", "mp"),
        P("req"),
        P("req", None, "mp"),
        P("req", None, None),
        P("req", "mp", None, None),
    )
    return jax.shard_map(
        shards,
        mesh=mesh,
        in_specs=placed,
        out_specs=(P("req", "seq", "mp"), P("req", "seq", "mp"), P("req", "seq", "mp", None, None)),
        check_vma=False,
    )
```

```python
import jax
import jax.numpy as jnp
from jax import lax
from jax.sharding import PartitionSpec as P
from jax.experimental import pallas as pl
from jax.experimental.pallas import tpu as pltpu

HD = 128
QH = 8
KVH = 2
NS = 256
CONV = 4


epsilon = 1e-05
rope_base = 100000000000.0
negative = -1e30


def shifted(block, axis, distance):
    devices = range(lax.axis_size(axis))
    route = [(i - distance, i) for i in devices if i - distance in devices]
    return lax.ppermute(block, axis, route)


def prefix(part, axis, combine, identity):
    place = lax.axis_index(axis)
    gathered = jax.tree.map(lambda a: lax.all_gather(a, axis), part)
    state = jax.tree.map(lambda a, e: jnp.zeros_like(a) + jnp.asarray(e, a.dtype), part, identity)

    def one(turn, state):
        return combine(
            state, jax.tree.map(lambda a: lax.dynamic_index_in_dim(a, turn, 0, False), gathered)
        )

    return lax.fori_loop(0, place, one, state)


def attend(query_rows, query_rank, pieces, key_rank, block):
    rows = query_rows.shape[0]
    count = pieces.shape[0]
    steps = count // block
    scale = 1.0 / float(HD) ** 0.5

    def kernel(qr_ref, q_ref, kr_ref, kv_ref, out_ref, top_ref, total_ref, acc_ref):
        step = pl.program_id(0)

        @pl.when(step == 0)
        def _():
            top_ref[...] = jnp.full(top_ref.shape, negative, jnp.float32)
            total_ref[...] = jnp.zeros(total_ref.shape, jnp.float32)
            acc_ref[...] = jnp.zeros(acc_ref.shape, jnp.float32)

        scores = lax.dot_general(
            q_ref[...], kv_ref[:, :HD], (((1,), (1,)), ((), ())), preferred_element_type=jnp.float32
        ) * scale
        valid = kr_ref[...] <= qr_ref[...]
        masked = jnp.where(valid, scores, negative)
        old = top_ref[...]
        new = jnp.maximum(old, jnp.max(masked, axis=1, keepdims=True))
        weights = jnp.where(valid, jnp.exp(masked - new), 0.0)
        alpha = jnp.exp(old - new)
        total_ref[...] = alpha * total_ref[...] + jnp.sum(weights, axis=1, keepdims=True)
        acc_ref[...] = alpha * acc_ref[...] + jnp.dot(
            weights.astype(jnp.bfloat16), kv_ref[:, HD:], preferred_element_type=jnp.float32
        )
        top_ref[...] = new

        @pl.when(step == steps - 1)
        def _():
            out_ref[...] = (acc_ref[...] / total_ref[...]).astype(out_ref.dtype)

    return pl.pallas_call(
        kernel,
        grid=(steps,),
        in_specs=[
            pl.BlockSpec((rows, 1), lambda i: (0, 0)),
            pl.BlockSpec((rows, HD), lambda i: (0, 0)),
            pl.BlockSpec((1, block), lambda i: (0, i)),
            pl.BlockSpec((block, 2 * HD), lambda i: (i, 0)),
        ],
        out_specs=pl.BlockSpec((rows, HD), lambda i: (0, 0)),
        out_shape=jax.ShapeDtypeStruct((rows, HD), jnp.bfloat16),
        scratch_shapes=[
            pltpu.VMEM((rows, 1), jnp.float32),
            pltpu.VMEM((rows, 1), jnp.float32),
            pltpu.VMEM((rows, HD), jnp.float32),
        ],
        compiler_params=pltpu.CompilerParams(vmem_limit_bytes=48 * 1024 * 1024),
    )(query_rank, query_rows, key_rank, pieces)


def rotate(values, positions):
    half = HD // 2
    freqs = rope_base ** (-jnp.arange(half, dtype=jnp.float32) * 2.0 / HD)
    angles = positions.astype(jnp.float32)[:, None] * freqs[None, :]
    cosine = jnp.cos(angles)[:, None, :]
    sine = jnp.sin(angles)[:, None, :]
    first = values[..., :half]
    second = values[..., half:]
    return jnp.concatenate(
        [first * cosine - second * sine, second * cosine + first * sine], axis=-1
    )


def rms_scale(values):
    mean_sq = jnp.mean(values * values, axis=-1, keepdims=True)
    return values * lax.rsqrt(mean_sq + epsilon)


def causal_conv(tail, inputs, taps):
    padded = jnp.concatenate([tail, inputs], axis=0).astype(jnp.float32)
    count = inputs.shape[0]
    total = jnp.zeros(inputs.shape, jnp.float32)
    for offset in range(CONV):
        total = total + taps[offset].astype(jnp.float32)[None, :] * padded[offset : offset + count]
    return jax.nn.silu(total)


def join_states(earlier, later):
    return (earlier[0] * later[0], later[0][:, None, None] * earlier[1] + later[1])


def shards(
    hidden,
    norm_gain,
    w_query,
    w_keyval,
    w_attn_out,
    w_inner,
    w_bc,
    w_dt,
    dt_bias,
    a_log,
    d_skip,
    conv_x,
    conv_bc,
    mamba_gain,
    w_mamba_out,
    cache,
    cache_len,
    tail_x,
    tail_bc,
    ssm_init,
):
    high = lax.Precision.HIGHEST
    own_rows = hidden[0]
    tokens = own_rows.shape[0]
    seq_pos = lax.axis_index("seq")
    mp_pos = lax.axis_index("mp")
    length = cache_len[0]
    mp_count = lax.axis_size("mp")
    width = own_rows.shape[1]
    whole = jnp.zeros((tokens, mp_count * width), own_rows.dtype)
    for shift in range(mp_count):
        if shift == 0:
            part = own_rows
        else:
            part = lax.ppermute(own_rows, "mp", [(i, (i + shift) % mp_count) for i in range(mp_count)])
        source = (lax.axis_index("mp") + mp_count - shift) % mp_count
        whole = lax.dynamic_update_slice(whole, part, (0, source * width))
    normed = (rms_scale(whole.astype(jnp.float32)) * norm_gain.astype(jnp.float32)).astype(
        jnp.bfloat16
    )
    positions = length + seq_pos * tokens + jnp.arange(tokens, dtype=jnp.int32)
    local_heads = w_query.shape[1] // HD
    query = rotate(
        jnp.dot(normed, w_query, preferred_element_type=jnp.float32).reshape(
            tokens, local_heads, HD
        ),
        positions,
    ).astype(jnp.bfloat16)
    projected = jnp.dot(normed, w_keyval, preferred_element_type=jnp.float32)
    roped = rotate(projected[:, None, :], positions)[:, 0, :]
    kv_block = jnp.where(mp_pos % 2 == 0, roped, projected).astype(jnp.bfloat16)
    bc_block = jnp.dot(normed, w_bc, preferred_element_type=jnp.float32).astype(jnp.bfloat16)
    bc_all = lax.all_gather(bc_block, "mp", axis=1, tiled=True)
    own_rows_kv = jnp.concatenate([cache[0], kv_block], axis=0)
    mp_size = lax.axis_size("mp")
    partner = lax.ppermute(own_rows_kv, "mp", [(i, i ^ 1) for i in range(mp_size)])
    is_key_block = mp_pos % 2 == 0
    group_rows = jnp.where(
        is_key_block,
        jnp.concatenate([own_rows_kv, partner], axis=1),
        jnp.concatenate([partner, own_rows_kv], axis=1),
    )
    inner = jnp.einsum("td,dkc->tkc", normed, w_inner, preferred_element_type=jnp.float32).astype(
        jnp.bfloat16
    )
    rim = CONV - 1
    prev_x, prev_bc = shifted((inner[tokens - rim :, 1], bc_all[tokens - rim :]), "seq", 1)
    first_block = seq_pos == 0
    prev_x = jnp.where(first_block, tail_x[0], prev_x)
    prev_bc = jnp.where(first_block, tail_bc[0], prev_bc)
    mamba_heads = dt_bias.shape[0]
    x_conv = causal_conv(prev_x, inner[:, 1], conv_x).reshape(tokens, mamba_heads, HD)
    bc_conv = causal_conv(prev_bc, bc_all, conv_bc)
    b_mat = bc_conv[:, :NS]
    c_mat = bc_conv[:, NS:]
    step_size = jax.nn.softplus(jnp.dot(normed, w_dt, preferred_element_type=jnp.float32) + dt_bias)
    log_decay = -step_size * jnp.exp(a_log)[None, :]
    cumulative = jnp.cumsum(log_decay, axis=0)
    pairs = jnp.dot(c_mat, b_mat.T, precision=high)
    gap = cumulative[:, None, :] - cumulative[None, :, :]
    token_ids = jnp.arange(tokens)
    lower = (token_ids[:, None] >= token_ids[None, :])[:, :, None]
    decay = jnp.where(lower, jnp.exp(jnp.where(lower, gap, 0.0)), 0.0)
    mixing = decay * pairs[:, :, None] * step_size[None, :, :]
    inner_out = jnp.einsum("tsh,shp->thp", mixing, x_conv, precision=high)
    to_end = jnp.exp(cumulative[-1][None, :] - cumulative) * step_size
    own_state = jnp.einsum("sh,shp,sn->hpn", to_end, x_conv, b_mat, precision=high)
    block_decay = jnp.exp(cumulative[-1])
    seq_size = lax.axis_size("seq")
    rows = HD // seq_size
    pieces = jnp.transpose(own_state.reshape(mamba_heads, seq_size, rows, NS), (1, 0, 2, 3))
    decays = jnp.broadcast_to(block_decay[None, :, None, None], (seq_size, mamba_heads, 1, NS))
    columns = lax.all_to_all(jnp.concatenate([pieces, decays], axis=2), "seq", 0, 0, tiled=True)
    carry = lax.dynamic_slice_in_dim(ssm_init[0], seq_pos * rows, rows, 1)
    entering = []
    for source in range(seq_size):
        entering.append(carry)
        part = columns[source]
        carry = part[:, rows:, :] * carry + part[:, :rows, :]
    entering = lax.all_to_all(jnp.stack(entering, axis=0), "seq", 0, 0, tiled=True)
    incoming = jnp.transpose(entering, (1, 0, 2, 3)).reshape(mamba_heads, HD, NS)
    carried = jnp.exp(cumulative)[:, :, None] * jnp.einsum(
        "tn,hpn->thp", c_mat, incoming, precision=high
    )
    mamba_y = inner_out + carried + d_skip[None, :, None] * x_conv
    state_after = block_decay[:, None, None] * incoming + own_state
    gated = mamba_y * jax.nn.silu(inner[:, 0].astype(jnp.float32).reshape(tokens, mamba_heads, HD))
    mixed = (
        rms_scale(gated).reshape(tokens, mamba_heads * HD) * mamba_gain.astype(jnp.float32)
    ).astype(jnp.bfloat16)
    cache_rows = cache.shape[1]
    shard_rows = cache_rows + tokens
    group = mp_pos * local_heads // (QH // KVH)
    query_index = seq_pos * tokens + jnp.arange(tokens, dtype=jnp.int32)
    scale = 1.0 / float(HD) ** 0.5
    piece = lax.all_gather(group_rows, "seq", axis=0, tiled=True)
    count = piece.shape[0]
    index = jnp.arange(count, dtype=jnp.int32)
    owner = index // shard_rows
    offset = index % shard_rows
    in_cache = offset < cache_rows
    slot_ok = in_cache & (owner * cache_rows + offset < length)
    new_index = owner * tokens + offset - cache_rows
    never = jnp.iinfo(jnp.int32).max
    key_rank = jnp.where(in_cache, jnp.where(slot_ok, -1, never), new_index)[None, :]
    query_rank = jnp.tile(query_index, local_heads)[:, None]
    query_rows = jnp.transpose(query, (1, 0, 2)).reshape(local_heads * tokens, HD)
    attended = attend(query_rows, query_rank, piece, key_rank, 8 * shard_rows)
    attended = jnp.transpose(attended.reshape(local_heads, tokens, HD), (1, 0, 2)).reshape(
        tokens, local_heads * HD
    )
    attended = attended.astype(jnp.bfloat16)
    mp_count = lax.axis_size("mp")
    out_cols = w_attn_out.shape[1] // mp_count
    attn_cols = lax.all_to_all(
        w_attn_out.reshape(w_attn_out.shape[0], mp_count, out_cols), "mp", 1, 0, tiled=True
    ).reshape(w_attn_out.shape[0] * mp_count, out_cols)
    mamba_term = jnp.dot(mixed, w_mamba_out, preferred_element_type=jnp.float32)
    summed = lax.psum_scatter(mamba_term.astype(jnp.bfloat16), "mp", scatter_dimension=1, tiled=True)
    head_cols = attended.shape[1]
    attended_all = jnp.zeros((tokens, mp_count * head_cols), attended.dtype)
    for shift in range(mp_count):
        if shift == 0:
            part = attended
        else:
            part = lax.ppermute(attended, "mp", [(i, (i + shift) % mp_count) for i in range(mp_count)])
        source = (mp_pos + mp_count - shift) % mp_count
        attended_all = lax.dynamic_update_slice(attended_all, part, (0, source * head_cols))
    summed = summed.astype(jnp.float32) + jnp.dot(
        attended_all, attn_cols, preferred_element_type=jnp.float32
    )
    layer = (summed + own_rows.astype(jnp.float32)).astype(jnp.bfloat16)
    return (layer[None], kv_block[None], state_after[None, None])


def solution(mesh):
    placed = (
        P("req", "seq", "mp"),
        P(),
        P(None, "mp"),
        P(None, "mp"),
        P("mp", None),
        P(None, None, "mp"),
        P(None, "mp"),
        P(None, "mp"),
        P("mp"),
        P("mp"),
        P("mp"),
        P(None, "mp"),
        P(),
        P("mp"),
        P("mp", None),
        P("req", "seq", "mp"),
        P("req"),
        P("req", None, "mp"),
        P("req", None, None),
        P("req", "mp", None, None),
    )
    return jax.shard_map(
        shards,
        mesh=mesh,
        in_specs=placed,
        out_specs=(P("req", "seq", "mp"), P("req", "seq", "mp"), P("req", "seq", "mp", None, None)),
        check_vma=False,
    )
```
